128 devices in a mesh: dom: 128 (over x, y, z, core).
Axes of the slice: x: 4, y: 4, z: 4, core: 2. Of those that a mesh axis runs over, the one named last changes fastest.
Arguments:
- state: float32 [9, 56, 49152], P(None, None, 'dom'), may hold values from -18 to 18
- class_label: int32 [49152], P('dom'), may hold values from 0 to 2, as said below
- stiffness: float32 [3, 56, 56], replicated, may hold values from -0.8 to 0.8
- star: float32 [3, 9, 9, 49152], P(None, None, None, 'dom'), may hold values from -0.84 to 0.84
- face_proj: float32 [4, 21, 56], replicated, may hold values from -0.75 to 0.75
- orient_map: float32 [3, 21, 21], replicated, may hold values from -1.25 to 1.25
- flux_local: float32 [4, 9, 9, 49152], P(None, None, None, 'dom'), may hold values from -0.12 to 0.15
- flux_neigh: float32 [4, 9, 9, 49152], P(None, None, None, 'dom'), may hold values from -0.12 to 0.12
- neighbor: int32 [4, 49152], P(None, 'dom'), may hold values from 0 to 1151, as said below
- neighbor_face: int32 [4, 49152], P(None, 'dom'), may hold values from 0 to 3
- orientation: int32 [4, 49152], P(None, 'dom'), may hold values from 0 to 2
- send_list: int32 [3072, 32], P('dom'), may hold values from -1 to 383, as said below
Outputs:
- final_state: float32 [9, 56, 49152], P(None, None, 'dom')
- energy: float32 [1], replicated
The draws below stay inside these ranges and needn't reach their ends.
Inputs may be any that keep to these rules, and one draw needn't show every extreme that they name: `class_label`: each device's block of 384 elements holds exactly 128 elements of each class 0, 1 and 2. `send_list`: row 3 (2 * 4 d + p) + g lists the local elements of device d sent to its bordering partition p for that partition's elements of class g: distinct indices followed by -1 for unused slots, at least one slot used; every device receives one row with all 32 slots used. `neighbor`: A value under 384 is another element of the same device; a value 384 + (3 p + g) * 32 + r names slot r of the row that bordering partition p sends for class g, stands only on faces of class-g elements, always names a used slot, and every used slot is named by exactly one face.
All inputs are finite; a program needn't handle non-finite values.
Results may differ from the reference program's by a relative error of at most 0.0001.
Values sent between devices are 32-bit elements; how exact they have to be, the bound alone decides.
No kernel may reach another device: no remote copies, remote signals or barrier semaphores. Data moves between devices by JAX's collectives and lax.ppermute only.
A program may use at most 256 MiB of HBM per device.

```python
import math
import jax
import jax.numpy as jnp
from jax import lax

BASIS = 56
QUANT = 9
FACE_BASIS = 21
ORDER = 6
REACH = 4
SLOTS = 32
CYCLES = 1
CLS_DEV = 128
ELEM_DEV = 384
ELEMS = 49152
PEERS = 8
GHOSTS = 768
N_DOM = 128


def labels_helper(key):
    base = jax.random.fold_in(key, 101)
    keys = jax.random.split(base, N_DOM)
    perms = jax.vmap(lambda single: jax.random.permutation(single, ELEM_DEV))(keys)
    return (perms // CLS_DEV).reshape(ELEMS).astype(jnp.int32)


def class_scale(key):
    labels = labels_helper(key)
    return jnp.where(labels == 0, 1.0, jnp.where(labels == 1, 0.5, 0.25)).astype(jnp.float32)


def topology(key):
    base = jax.random.fold_in(key, 202)
    first, second, third = jax.random.split(base, 3)
    counts = jax.random.randint(first, (N_DOM, PEERS * 3), 1, SLOTS + 1)
    full_row = jax.random.randint(second, (N_DOM,), 0, PEERS * 3)
    chosen_dev = jax.random.randint(third, (), 0, N_DOM)
    devs = jnp.arange(N_DOM)
    full_row = jnp.where(devs == chosen_dev, PEERS * 3 - 1, full_row)
    columns = jnp.arange(PEERS * 3)
    counts = jnp.where(columns[None, :] == full_row[:, None], SLOTS, counts)
    return counts.reshape(N_DOM, PEERS, 3).astype(jnp.int32)


def draw_class_label(key, part):
    return labels_helper(key)


def draw_state(key, part):
    base = jax.random.fold_in(key, 303)
    device_pos = (jnp.arange(ELEMS) // ELEM_DEV).astype(jnp.float32) / (N_DOM - 1)
    rising = 1.0 + 2.0 * device_pos
    values = jnp.clip(jax.random.normal(base, (QUANT, BASIS, ELEMS), jnp.float32), -6.0, 6.0)
    values = values * rising
    return values.astype(jnp.float32)


def draw_stiffness(key, part):
    base = jax.random.fold_in(key, 404)
    raw = jnp.clip(jax.random.normal(base, (3, BASIS, BASIS), jnp.float32), -4.0, 4.0) * 0.095
    return (raw - jnp.transpose(raw, (0, 2, 1))).astype(jnp.float32)


def draw_star(key, part):
    base = jax.random.fold_in(key, 505)
    raw = jnp.clip(jax.random.normal(base, (3, QUANT, QUANT, ELEMS), jnp.float32), -4.0, 4.0) * 0.104
    symmetric = raw + jnp.transpose(raw, (0, 2, 1, 3))
    return (symmetric * class_scale(key)[None, None, None, :]).astype(jnp.float32)


def draw_flux_local(key, part):
    base = jax.random.fold_in(key, 606)
    first, second = jax.random.split(base)
    raw = jnp.clip(jax.random.normal(first, (4, QUANT, QUANT, ELEMS), jnp.float32), -4.0, 4.0) * 0.015
    diagonal = jax.random.uniform(second, (4, QUANT, 1, ELEMS), jnp.float32, 0.05, 0.15)
    eye = (jnp.arange(QUANT)[:, None] == jnp.arange(QUANT)[None, :]).astype(jnp.float32)[None, :, :, None]
    off = (raw + jnp.transpose(raw, (0, 2, 1, 3))) * (1.0 - eye)
    matrix = off + eye * diagonal
    return (matrix * class_scale(key)[None, None, None, :]).astype(jnp.float32)


def draw_flux_neigh(key, part):
    base = jax.random.fold_in(key, 707)
    raw = jnp.clip(jax.random.normal(base, (4, QUANT, QUANT, ELEMS), jnp.float32), -4.0, 4.0) * 0.03
    return (raw * class_scale(key)[None, None, None, :]).astype(jnp.float32)


def draw_send_list(key, part):
    counts = topology(key)
    peer_ids = jnp.arange(PEERS)
    offsets = jnp.where(peer_ids < REACH, peer_ids - REACH, peer_ids - REACH + 1)
    devs = jnp.arange(N_DOM)
    receiver = (devs[:, None] + offsets[None, :]) % N_DOM
    used = counts[receiver, (PEERS - 1 - peer_ids)[None, :], :]
    keys = jax.random.split(jax.random.fold_in(key, 808), N_DOM * PEERS * 3)
    picks = jax.vmap(lambda single: jax.random.permutation(single, ELEM_DEV)[:SLOTS])(keys)
    picks = picks.reshape(N_DOM, PEERS, 3, SLOTS)
    slot_ids = jnp.arange(SLOTS)
    result = jnp.where(slot_ids[None, None, None, :] < used[:, :, :, None], picks, -1)
    return result.reshape(N_DOM * PEERS * 3, SLOTS).astype(jnp.int32)


def place_ghosts(row, spots, used_dev, labels_dev):
    face_labels = jnp.tile(labels_dev, 4)
    shifted = 4 * ELEM_DEV
    peer_ids = jnp.arange(PEERS, dtype=jnp.int32)[:, None]
    slot_ids = jnp.arange(SLOTS, dtype=jnp.int32)[None, :]
    for category in range(3):
        score = jnp.where(face_labels == category, spots, spots + shifted)
        chosen = jnp.argsort(score)[:PEERS * SLOTS]
        ghost_ids = (ELEM_DEV + (peer_ids * 3 + category) * SLOTS + slot_ids).reshape(PEERS * SLOTS).astype(jnp.int32)
        fresh = jnp.where(used_dev[:, category, :].reshape(PEERS * SLOTS), ghost_ids, row[chosen])
        row = row.at[chosen].set(fresh)
    return row


def draw_neighbor(key, part):
    counts = topology(key)
    used = jnp.arange(SLOTS)[None, None, None, :] < counts[:, :, :, None]
    labels = labels_helper(key).reshape(N_DOM, ELEM_DEV)
    base = jax.random.fold_in(key, 909)
    first, second = jax.random.split(base)
    elem_ids = jnp.arange(ELEM_DEV)
    steps_away = jax.random.randint(first, (N_DOM, 4, ELEM_DEV), 1, ELEM_DEV)
    local = ((elem_ids[None, None, :] + steps_away) % ELEM_DEV).astype(jnp.int32)
    flat = local.reshape(N_DOM, 4 * ELEM_DEV)
    keys = jax.random.split(second, N_DOM)
    spots = jax.vmap(lambda single: jax.random.permutation(single, 4 * ELEM_DEV))(keys)
    flat = jax.vmap(place_ghosts)(flat, spots, used, labels)
    result = jnp.transpose(flat.reshape(N_DOM, 4, ELEM_DEV), (1, 0, 2)).reshape(4, ELEMS)
    return result.astype(jnp.int32)


def place_ends(values, own_key, low, high):
    shape = values.shape
    spot = [jax.random.randint(jax.random.fold_in(own_key, axis), (), 0, shape[axis]) for axis in range(len(shape))]
    values = values.at[tuple(spot)].set(low)
    longest = shape.index(max(shape))
    spot[longest] = (spot[longest] + 1) % shape[longest]
    return values.at[tuple(spot)].set(high)


def centred(key, extent, deviation, most, kind=jnp.bfloat16):
    return jnp.clip(deviation * jax.random.normal(key, extent, jnp.float32), -most, most).astype(kind)


def setup_inputs(seed: int = 0) -> dict:
    arg_keys = jax.random.split(jax.random.key(seed), 13)
    state = draw_state(jax.random.fold_in(arg_keys[12], 71), 0)
    class_label = draw_class_label(jax.random.fold_in(arg_keys[12], 71), 0)
    stiffness = draw_stiffness(jax.random.fold_in(arg_keys[12], 71), 0)
    star = draw_star(jax.random.fold_in(arg_keys[12], 71), 0)
    face_proj = centred(arg_keys[4], (4, FACE_BASIS, BASIS), BASIS ** -0.5, 0.75, jnp.float32)
    orient_map = centred(arg_keys[5], (3, FACE_BASIS, FACE_BASIS), FACE_BASIS ** -0.5, 1.25, jnp.float32)
    flux_local = draw_flux_local(jax.random.fold_in(arg_keys[12], 71), 0)
    flux_neigh = draw_flux_neigh(jax.random.fold_in(arg_keys[12], 71), 0)
    neighbor = draw_neighbor(jax.random.fold_in(arg_keys[12], 71), 0)
    neighbor_face = place_ends(jax.random.randint(arg_keys[9], (4, ELEMS), 0, 4), jax.random.fold_in(arg_keys[9], 1), 0, 3).astype(jnp.int32)
    orientation = place_ends(jax.random.randint(arg_keys[10], (4, ELEMS), 0, 3), jax.random.fold_in(arg_keys[10], 1), 0, 2).astype(jnp.int32)
    send_list = draw_send_list(jax.random.fold_in(arg_keys[12], 71), 0)
    return {"state": state, "class_label": class_label, "stiffness": stiffness, "star": star, "face_proj": face_proj, "orient_map": orient_map, "flux_local": flux_local, "flux_neigh": flux_neigh, "neighbor": neighbor, "neighbor_face": neighbor_face, "orientation": orientation, "send_list": send_list}


HIGH = lax.Precision.HIGHEST


def element_mix(matrix, values):
    total = None
    for q in range(matrix.shape[1]):
        term = matrix[:, q, None, :] * values[q][None, :, :]
        total = term if total is None else total + term
    return total


def apply_star(values, stiffness, star):
    total = None
    for d in range(3):
        moved = jnp.einsum('ab,qbe->qae', stiffness[d], values, precision=HIGH)
        term = element_mix(star[d], moved)
        total = term if total is None else total + term
    return total


def predict(values, stiffness, star):
    derivs = [values]
    for k in range(ORDER - 1):
        derivs.append(apply_star(derivs[-1], stiffness, star))
    return derivs


def integrate(derivs, start):
    total = None
    for k in range(ORDER):
        weight = ((start + 1.0) ** (k + 1) - float(start) ** (k + 1)) / math.factorial(k + 1)
        term = derivs[k] * weight
        total = term if total is None else total + term
    return total


def correct(values, own, near, near_face, near_orient, stiffness, star, face_proj, orient_map, flux_local, flux_neigh):
    update = apply_star(own, stiffness, star)
    for f in range(4):
        on_face = jnp.einsum('ab,qbe->qae', face_proj[f], own, precision=HIGH)
        lifted = jnp.einsum('ba,qbe->qae', face_proj[f], on_face, precision=HIGH)
        update = update - element_mix(flux_local[f], lifted)
        chosen = None
        for j in range(4):
            projected = jnp.einsum('ab,qbe->qae', face_proj[j], near[:, :, f, :], precision=HIGH)
            term = jnp.where((near_face[f] == j)[None, None, :], projected, 0.0)
            chosen = term if chosen is None else chosen + term
        aligned = None
        for h in range(3):
            turned = jnp.einsum('ab,qbe->qae', orient_map[h], chosen, precision=HIGH)
            term = jnp.where((near_orient[f] == h)[None, None, :], turned, 0.0)
            aligned = term if aligned is None else aligned + term
        lifted_near = jnp.einsum('ba,qbe->qae', face_proj[f], aligned, precision=HIGH)
        update = update - element_mix(flux_neigh[f], lifted_near)
    return values + update


def reference(state, class_label, stiffness, star, face_proj, orient_map, flux_local, flux_neigh, neighbor, neighbor_face, orientation, send_list):
    offsets = [p - REACH if p < REACH else p - REACH + 1 for p in range(PEERS)]
    devs = jnp.arange(N_DOM, dtype=jnp.int32)
    blocks = send_list.reshape(N_DOM, PEERS, 3, SLOTS)
    columns = []
    for p in range(PEERS):
        source = (devs + offsets[p]) % N_DOM
        local_rows = blocks[source, PEERS - 1 - p]
        columns.append((source[:, None, None] * ELEM_DEV + jnp.maximum(local_rows, 0)).reshape(N_DOM, 3 * SLOTS))
    ghost_global = jnp.concatenate(columns, axis=1).astype(jnp.int32)
    nbr = neighbor.reshape(4, N_DOM, ELEM_DEV)
    owner = devs[None, :, None]
    ghost_hit = ghost_global[owner, jnp.clip(nbr - ELEM_DEV, 0, GHOSTS - 1)]
    nbr_global = jnp.where(nbr < ELEM_DEV, owner * ELEM_DEV + nbr, ghost_hit).reshape(4, ELEMS).astype(jnp.int32)
    class_order = jnp.argsort(class_label, stable=True).astype(jnp.int32)
    rank_of = jnp.argsort(class_order).astype(jnp.int32)
    near_index = rank_of[nbr_global[:, class_order]].reshape(-1)
    near_face = neighbor_face[:, class_order]
    near_orient = orientation[:, class_order]
    star_sorted = star[:, :, :, class_order]
    local_sorted = flux_local[:, :, :, class_order]
    neigh_sorted = flux_neigh[:, :, :, class_order]
    count = CLS_DEV * N_DOM
    sorted_state = state[:, :, class_order]
    fields = [sorted_state[:, :, c * count:(c + 1) * count] for c in range(3)]
    derivs = [None, None, None]
    owns = [None, None, None]
    nears = [None, None, None]
    energies = []
    for n in range(4 * CYCLES):
        pieces = []
        for c in range(3):
            span = 2 ** c
            window = slice(c * count, (c + 1) * count)
            if n % span == 0:
                derivs[c] = predict(fields[c], stiffness, star_sorted[:, :, :, window])
            pieces.append(integrate(derivs[c], n % span))
        current = jnp.concatenate(pieces, axis=2)
        gathered = jnp.take(current, near_index, axis=2).reshape(QUANT, BASIS, 4, ELEMS)
        for c in range(3):
            span = 2 ** c
            window = slice(c * count, (c + 1) * count)
            if n % span == 0:
                owns[c] = pieces[c]
                nears[c] = gathered[:, :, :, window]
            else:
                owns[c] = owns[c] + pieces[c]
                nears[c] = nears[c] + gathered[:, :, :, window]
            if (n + 1) % span == 0:
                fields[c] = correct(fields[c], owns[c], nears[c], near_face[:, window], near_orient[:, window], stiffness, star_sorted[:, :, :, window], face_proj, orient_map, local_sorted[:, :, :, window], neigh_sorted[:, :, :, window])
        if (n + 1) % 4 == 0:
            squares = jnp.sum(fields[0] * fields[0]) + jnp.sum(fields[1] * fields[1]) + jnp.sum(fields[2] * fields[2])
            energies.append(squares / (ELEMS * QUANT * BASIS))
    final_sorted = jnp.concatenate(fields, axis=2)
    final_state = final_sorted[:, :, rank_of]
    return final_state, jnp.stack(energies)
```

```python
import math

import jax
import jax.numpy as jnp
from jax import lax
from jax.experimental import pallas as pl
from jax.experimental.pallas import tpu as pltpu
from jax.sharding import PartitionSpec as P

ORDER = 6
Q = 9
B = 56
FB = 21
FP = 24
L = 128
REACH = 4
PEERS = 8
SLOTS = 32
GROUP = 8
STEPS = 4
OFFSETS = [p - REACH if p < REACH else p - REACH + 1 for p in range(PEERS)]
KROWS = 3 * B
WROWS = KROWS + 4 * FP
MSG = 7
F32 = jnp.float32
BF16 = jnp.bfloat16
I32 = jnp.int32
VMEM_LIMIT = 40 * 1024 * 1024


def shape(dims, dtype=F32):
    return jax.ShapeDtypeStruct(dims, dtype)


def call(kernel, outs, scratch, name):
    return pl.pallas_call(
        kernel,
        out_shape=outs,
        scratch_shapes=scratch,
        compiler_params=pltpu.CompilerParams(vmem_limit_bytes=VMEM_LIMIT),
        name=name,
    )


def lane_take(x, index):
    numbers = lax.GatherDimensionNumbers(
        offset_dims=(),
        collapsed_slice_dims=(1,),
        start_index_map=(1,),
        operand_batching_dims=(0,),
        start_indices_batching_dims=(0,),
    )
    return lax.gather(
        x,
        index[..., None],
        numbers,
        slice_sizes=(1, 1),
        mode=lax.GatherScatterMode.PROMISE_IN_BOUNDS,
    )


def pick(blocks, code, lane):
    out = lane_take(blocks[0], lane)
    for k in range(1, len(blocks)):
        out = jnp.where(code == k, lane_take(blocks[k], lane), out)
    return out


def rows_of(vec, rows):
    return jnp.broadcast_to(vec, (rows, L))


def split(values):
    hi = values.astype(BF16)
    lo = (values - hi.astype(F32)).astype(BF16)
    return hi, lo


def put_stack(ref, q, values, rows):
    have = values.shape[0]
    if have < rows:
        values = jnp.concatenate([values, jnp.zeros((rows - have, L), F32)], axis=0)
    hi, lo = split(values)
    cols = slice(q * L, (q + 1) * L)
    ref[0:rows, cols] = hi
    ref[rows : 2 * rows, cols] = lo
    ref[2 * rows : 3 * rows, cols] = hi


def column_tiles():
    return [(t, min(2, Q - t)) for t in range(0, Q, 2)]


def product(weights, stack_ref, store, contract=1):
    for start, count in column_tiles():
        cols = slice(start * L, (start + count) * L)
        out = lax.dot_general(
            weights,
            stack_ref[:, cols],
            (((contract,), (0,)), ((), ())),
            preferred_element_type=F32,
        )
        for j in range(count):
            store(start + j, out[:, j * L : (j + 1) * L])


def mix_groups(total, most):
    groups = []
    at = 0
    while at < total:
        size = min(most, total - at)
        groups.append((at, size))
        at += size
    return groups


def row_bcast(ref, at, q):
    return ref[at, pl.ds(q, 8, stride=0), :][None]


def star_mix(star_ref, moved_ref, put):
    for r0, rn in mix_groups(B, 32):
        acc = [None] * Q
        for d in range(3):
            for q in range(Q):
                m = moved_ref[q, d * B + r0 : d * B + r0 + rn, :].reshape(rn // 8, 8, L)
                for p in range(Q):
                    term = row_bcast(star_ref, d * Q + p, q) * m
                    acc[p] = term if acc[p] is None else acc[p] + term
        for p in range(Q):
            put(p, r0, rn, acc[p].reshape(rn, L))


def class_lanes(c):
    return slice(c * L, (c + 1) * L)


def nt_dot(a, b):
    return lax.dot_general(a, b, (((1,), (1,)), ((), ())), preferred_element_type=F32)


def index_kernel(
    dev_ref, label_ref, nbr_ref, face_ref, orient_ref, send_ref, stiff_ref, proj_ref, omap_ref,
    order_ref, rank_ref, code_ref, lane_ref, sorted_orient_ref, send_blk_ref, send_lane_ref,
    req_a_ref, req_b_ref, w_ref, ow_ref, lw_ref,
    wf_ref, owf_ref, lwf_ref,
):
    n_el = label_ref.shape[1]
    wf_ref[...] = jnp.zeros_like(wf_ref)
    owf_ref[...] = jnp.zeros_like(owf_ref)
    for d in range(3):
        k = stiff_ref[d]
        hi = k.astype(BF16).astype(F32)
        rows = slice(d * B, (d + 1) * B)
        wf_ref[rows, 0:B] = hi
        wf_ref[rows, 64 : 64 + B] = hi
        wf_ref[rows, 128 : 128 + B] = k - hi
    lwf_ref[...] = jnp.zeros_like(lwf_ref)
    for j in range(4):
        k = proj_ref[j]
        hi = k.astype(BF16).astype(F32)
        rows = slice(KROWS + j * FP, KROWS + j * FP + FB)
        wf_ref[rows, 0:B] = hi
        wf_ref[rows, 64 : 64 + B] = hi
        wf_ref[rows, 128 : 128 + B] = k - hi
        lwf_ref[j * FP : j * FP + FB, :] = hi
        lwf_ref[96 + j * FP : 96 + j * FP + FB, :] = hi
        lwf_ref[192 + j * FP : 192 + j * FP + FB, :] = k - hi
    for h in range(3):
        k = omap_ref[h]
        hi = k.astype(BF16).astype(F32)
        rows = slice(h * FP, h * FP + FB)
        owf_ref[rows, 0:FB] = hi
        owf_ref[rows, 32 : 32 + FB] = hi
        owf_ref[rows, 64 : 64 + FB] = k - hi
    w_ref[...] = wf_ref[...].astype(BF16)
    ow_ref[...] = owf_ref[...].astype(BF16)
    lw_ref[...] = lwf_ref[...].astype(BF16)
    label = label_ref[...]
    classes = lax.broadcasted_iota(I32, (8, n_el), 0)
    hot = (jnp.broadcast_to(label, (8, n_el)) == classes).astype(F32)
    row = lax.broadcasted_iota(I32, (n_el, n_el), 0)
    col = lax.broadcasted_iota(I32, (n_el, n_el), 1)
    before = (row < col).astype(F32).astype(BF16)
    prefix = jnp.dot(hot.astype(BF16), before, preferred_element_type=F32)
    base = classes.astype(F32) * float(L)
    rank = jnp.sum(hot * (prefix + base), axis=0, keepdims=True).astype(I32)
    here = (jnp.broadcast_to(rank, (n_el, n_el)) == row).astype(F32).astype(BF16)
    ids = lax.broadcasted_iota(I32, (8, n_el), 1)
    first = lax.broadcasted_iota(I32, (8, n_el), 0) == 0
    parts = jnp.where(first, ids // L, ids % L).astype(F32).astype(BF16)
    order = nt_dot(parts, here).astype(I32)
    order_ref[...] = order
    rank_ref[...] = jnp.where(first, jnp.broadcast_to(rank >> 7, (8, n_el)), jnp.broadcast_to(rank & 127, (8, n_el)))
    rank_blocks = [rows_of(rank[:, class_lanes(c)], 8) for c in range(3)]
    pad = jnp.zeros((4, n_el), I32)
    tables = [jnp.concatenate([ref[...], pad], axis=0) for ref in (nbr_ref, face_ref, orient_ref)]
    sub = lax.broadcasted_iota(I32, (8, L), 0)
    lanes = lax.broadcasted_iota(I32, (8, L), 1)
    for c in range(3):
        blk = rows_of(order[0:1, class_lanes(c)], 8)
        lane = rows_of(order[1:2, class_lanes(c)], 8)
        nbr, face, orient = [
            pick([t[:, class_lanes(b)] for b in range(3)], blk, lane) for t in tables
        ]
        ghost = nbr >= n_el
        inside = jnp.where(ghost, 0, nbr)
        place = pick(rank_blocks, inside >> 7, inside & 127)
        slot = jnp.where(ghost, nbr - n_el, 0)
        peer = ((slot >> 5) * 11) >> 5
        slot = peer * SLOTS + (slot & 31)
        code_ref[c] = jnp.where(ghost, 12 + (slot >> 7), face * 3 + (place >> 7))
        lane_ref[c] = jnp.where(ghost, slot & 127, place & 127)
        sorted_orient_ref[c] = orient
        slot = jnp.where(ghost, slot, -1)
        want = jnp.zeros((8, 2 * L), F32)
        target = lax.broadcasted_iota(I32, (2 * L, L), 0)
        for f in range(4):
            match = (jnp.broadcast_to(slot[f : f + 1], (2 * L, L)) == target).astype(F32).astype(BF16)
            value = rows_of(face[f : f + 1], 8).astype(F32).astype(BF16)
            want = want + nt_dot(value, match)
        want = want.astype(I32)
        for p in range(PEERS):
            half = want[:, class_lanes(p // 4)]
            turn = (-(p % 4) * SLOTS) % L
            moved = pltpu.roll(half, turn, axis=1) if turn else half
            wf_ref[8 * p : 8 * p + 8, 0:L] = jnp.where(
                sub == c, moved.astype(F32), wf_ref[8 * p : 8 * p + 8, 0:L]
            )
    place_in_group = dev_ref[0] % GROUP
    other_place = (place_in_group + REACH) % GROUP
    for p in range(PEERS):
        message = wf_ref[8 * p : 8 * p + 8, 0:L].astype(I32)
        to = place_in_group + OFFSETS[p]
        within = jnp.logical_and(to >= 0, to < GROUP)

        @pl.when(within)
        def _():
            req_a_ref[jnp.where(within, to, 0)] = message

        @pl.when(jnp.logical_not(within))
        def _():
            req_b_ref[jnp.where(within, 0, other_place + OFFSETS[p])] = message

    send = jnp.maximum(send_ref[...], 0)
    place = pick(rank_blocks, send >> 7, send & 127)
    send_blk_ref[...] = place >> 7
    send_lane_ref[...] = place & 127


def run_steps(count, star_ref, d_ref, w_ref, stack_ref, moved_ref):
    def body(k, carry):
        for q in range(Q):
            put_stack(stack_ref, q, d_ref[k, q], 64)

        def store(q, out):
            moved_ref[q, 0:KROWS] = out

        product(w_ref[0:KROWS, :], stack_ref, store)

        def put(p, r0, rn, value):
            d_ref[k + 1, p, r0 : r0 + rn, :] = value

        star_mix(star_ref, moved_ref, put)
        return carry

    lax.fori_loop(0, count, body, 0)


def weights_between(start, end):
    return [(float(end) ** (k + 1) - float(start) ** (k + 1)) / math.factorial(k + 1) for k in range(ORDER)]


def integrate(d_ref, q, start, end):
    total = None
    for k, weight in enumerate(weights_between(start, end)):
        term = d_ref[k, q] * weight
        total = term if total is None else total + term
    return total


def traces(d_ref, w_ref, stack_ref, start, trace_ref):
    for q in range(Q):
        put_stack(stack_ref, q, integrate(d_ref, q, start, start + 1), 64)

    def store(q, out):
        trace_ref[q] = out

    product(w_ref[KROWS:WROWS, :], stack_ref, store)


def after_steps(c, d_ref, w_ref, stack_ref, own_ref, trace_refs):
    span = 2**c
    for t in range(span):
        traces(d_ref, w_ref, stack_ref, t, trace_refs[t])
    for q in range(Q):
        own_ref[q] = integrate(d_ref, q, 0, span)


def block_transpose(four, lane):
    a, b, c, d = four
    low = (lane & 64) == 0
    a, c = jnp.where(low, a, pltpu.roll(c, 64, axis=1)), jnp.where(low, pltpu.roll(a, 64, axis=1), c)
    b, d = jnp.where(low, b, pltpu.roll(d, 64, axis=1)), jnp.where(low, pltpu.roll(b, 64, axis=1), d)
    low = (lane & 32) == 0
    a, b = jnp.where(low, a, pltpu.roll(b, 32, axis=1)), jnp.where(low, pltpu.roll(a, 96, axis=1), b)
    c, d = jnp.where(low, c, pltpu.roll(d, 32, axis=1)), jnp.where(low, pltpu.roll(c, 96, axis=1), d)
    return [a, b, c, d]


def tile_at(v, k):
    t = MSG * k + v
    return (t // 3, t % 3) if t < 3 * Q else None


def pack(dev_ref, rows, req_ref, send_blk_ref, send_lane_ref, gat_ref, msg_ref, out_a_ref, out_b_ref):
    place_in_group = dev_ref[0] % GROUP
    other_place = (place_in_group + REACH) % GROUP
    lane = lax.broadcasted_iota(I32, (8, L), 1)
    for at, (g, sources) in enumerate(rows):
        for half in range(2):
            row = 2 * g + half
            code = req_ref[row : row + 1] * 3 + send_blk_ref[row : row + 1]
            code = rows_of(code, FP)
            index = rows_of(send_lane_ref[row : row + 1], FP)

            def body(q, carry):
                blocks = [sources[k % 3][q, (k // 3) * FP : (k // 3) * FP + FP, :] for k in range(12)]
                gat_ref[q] = pick(blocks, code, index)
                return carry

            lax.fori_loop(0, Q, body, 0)
            for v in range(MSG):
                four = []
                for k in range(4):
                    t = tile_at(v, k)
                    if t is None:
                        four.append(jnp.zeros((8, L), F32))
                    else:
                        four.append(gat_ref[t[0], 8 * t[1] : 8 * t[1] + 8, :])
                for k, value in enumerate(block_transpose(four, lane)):
                    msg_ref[4 * half + k, v] = value
        for p in range(PEERS):
            to = place_in_group + OFFSETS[p]
            within = jnp.logical_and(to >= 0, to < GROUP)

            @pl.when(within)
            def _():
                out_a_ref[jnp.where(within, to, 0), at] = msg_ref[p]

            @pl.when(jnp.logical_not(within))
            def _():
                out_b_ref[jnp.where(within, 0, other_place + OFFSETS[p]), at] = msg_ref[p]


def unpack(dev_ref, at, got_a_ref, got_b_ref, ghost_ref):
    place_in_group = dev_ref[0] % GROUP
    other_place = (place_in_group + REACH) % GROUP
    lane = lax.broadcasted_iota(I32, (8, L), 1)
    for half in range(2):
        found = []
        for k in range(4):
            at_group = place_in_group + OFFSETS[4 * half + k]
            within = jnp.logical_and(at_group >= 0, at_group < GROUP)
            first = got_a_ref[jnp.where(within, at_group, 0), at]
            second = got_b_ref[jnp.where(within, 0, other_place + OFFSETS[4 * half + k]), at]
            found.append(jnp.where(within, first, second))
        for v in range(MSG):
            moved = block_transpose([found[k][v] for k in range(4)], lane)
            for k in range(4):
                t = tile_at(v, k)
                if t is not None:
                    ghost_ref[half, t[0], 8 * t[1] : 8 * t[1] + 8, :] = moved[k]


def correct(
    state_ref, own_ref, sources, ghost_ref, code_ref, lane_ref, orient_ref, c,
    star_ref, fl_ref, fn_ref, w_ref, ow_ref, lw_ref,
    stack_ref, moved_ref, chosen_ref, cstack_ref, near_ref, flux_ref, fstack_ref, new_ref,
):
    for q in range(Q):
        put_stack(stack_ref, q, own_ref[q], 64)

    def store(q, out):
        moved_ref[q] = out

    product(w_ref[...], stack_ref, store)

    def put(p, r0, rn, value):
        new_ref[p, r0 : r0 + rn, :] = state_ref[p, r0 : r0 + rn, :] + value

    star_mix(star_ref, moved_ref, put)
    for f in range(4):
        code = rows_of(code_ref[c, f : f + 1, :], FP)
        index = rows_of(lane_ref[c, f : f + 1, :], FP)

        def body(q, carry):
            blocks = [sources[k % 3][q, (k // 3) * FP : (k // 3) * FP + FP, :] for k in range(12)]
            blocks += [ghost_ref[half, q] for half in range(2)]
            chosen_ref[q] = pick(blocks, code, index)
            return carry

        lax.fori_loop(0, Q, body, 0)
        for q in range(Q):
            put_stack(cstack_ref, q, chosen_ref[q], 32)
        turn = rows_of(orient_ref[c, f : f + 1, :], FP)

        def store_near(q, out):
            value = jnp.where(turn == 1, out[FP : 2 * FP], out[0:FP])
            near_ref[q, f * FP : (f + 1) * FP] = jnp.where(turn == 2, out[2 * FP :], value)

        product(ow_ref[...], cstack_ref, store_near)

    def flux_body(f, carry):
        acc = [None] * Q
        r = pl.multiple_of(f * FP, 8)
        for q in range(Q):
            mine = moved_ref[q, pl.ds(KROWS + r, FP), :].reshape(3, 8, L)
            theirs = near_ref[q, pl.ds(r, FP), :].reshape(3, 8, L)
            for p in range(Q):
                term = row_bcast(fl_ref, f * Q + p, q) * mine
                acc[p] = term if acc[p] is None else acc[p] + term
                acc[p] = acc[p] + row_bcast(fn_ref, f * Q + p, q) * theirs
        for p in range(Q):
            flux_ref[p, pl.ds(r, FP), :] = acc[p].reshape(FP, L)
        return carry

    lax.fori_loop(0, 4, flux_body, 0)
    for p in range(Q):
        put_stack(fstack_ref, p, flux_ref[p], 96)

    def subtract(p, out):
        new_ref[p] = new_ref[p] - out

    product(lw_ref[...], fstack_ref, subtract, contract=0)


def first_kernel(
    state_ref, star_ref, fl_ref, fn_ref, order_ref, w_ref,
    s_ref, star_out, fl_out, fn_out, own0, own1, own2, t00, t10, t11, t20, t21, t22, t23,
    d_ref, stack_ref, moved_ref,
):
    picks = []
    for c in range(3):
        picks.append((order_ref[0:1, class_lanes(c)], order_ref[1:2, class_lanes(c)]))

    def sort_rows(src, rows, put):
        blocks = [src[:, class_lanes(b)] for b in range(3)]
        for c in range(3):
            put(c, pick(blocks, rows_of(picks[c][0], rows), rows_of(picks[c][1], rows)))

    def sort_state(q, carry):
        def put(c, value):
            s_ref[c, q] = value
            d_ref[c, 0, q] = value

        sort_rows(state_ref[q], B, put)
        return carry

    lax.fori_loop(0, Q, sort_state, 0)

    def sort_matrix(src, dst, at, i, p):
        def put(c, value):
            dst[c, at, 0:Q, :] = value

        sort_rows(src[i, p], Q, put)

    def sort_star(p, carry):
        for d in range(3):
            sort_matrix(star_ref, star_out, d * Q + p, d, p)
        return carry

    lax.fori_loop(0, Q, sort_star, 0)

    def sort_flux(p, carry):
        for f in range(4):
            sort_matrix(fl_ref, fl_out, f * Q + p, f, p)
            sort_matrix(fn_ref, fn_out, f * Q + p, f, p)
        return carry

    lax.fori_loop(0, Q, sort_flux, 0)

    def each(c, carry):
        run_steps(ORDER - 1, star_out.at[c], d_ref.at[c], w_ref, stack_ref, moved_ref)
        return carry

    lax.fori_loop(0, 3, each, 0)
    after_steps(0, d_ref.at[0], w_ref, stack_ref, own0, [t00])
    after_steps(1, d_ref.at[1], w_ref, stack_ref, own1, [t10, t11])
    after_steps(2, d_ref.at[2], w_ref, stack_ref, own2, [t20, t21, t22, t23])


def first_pack_kernel(
    dev_ref, req_a_ref, req_b_ref, send_blk_ref, send_lane_ref, t0, t1, t2,
    req_ref, out_a_ref, out_b_ref,
    gat_ref, msg_ref,
):
    place_in_group = dev_ref[0] % GROUP
    other_place = (place_in_group + REACH) % GROUP
    lane = lax.broadcasted_iota(I32, (1, L), 1)
    rows = [jnp.zeros((1, L), I32) for _ in range(8)]
    for p in range(PEERS):
        at_group = place_in_group + OFFSETS[p]
        within = jnp.logical_and(at_group >= 0, at_group < GROUP)
        first = req_a_ref[jnp.where(within, at_group, 0)]
        second = req_b_ref[jnp.where(within, 0, other_place + OFFSETS[p])]
        message = jnp.where(within, first, second)
        turn = (p % 4) * SLOTS
        message = pltpu.roll(message, turn, axis=1) if turn else message
        part = (lane >> 5) == (p % 4)
        for g in range(3):
            row = 2 * g + p // 4
            rows[row] = jnp.where(part, message[g : g + 1], rows[row])
    for row in range(8):
        req_ref[row : row + 1] = rows[row]
    pack(dev_ref, [(0, [t0, t1, t2])], req_ref, send_blk_ref, send_lane_ref, gat_ref, msg_ref, out_a_ref, out_b_ref)


def step_kernel(n, *refs):
    refs = list(refs)

    def take(count):
        got = refs[:count]
        del refs[:count]
        return got

    ending = [c for c in range(3) if n % 2**c == 0]
    sending = [c for c in range(3) if (n + 1) % 2**c == 0] if n < STEPS else []
    last = n == STEPS
    (dev_ref, got_a, got_b, code_ref, lane_ref, orient_ref) = take(6)
    star_ref, fl_ref, fn_ref, w_ref, ow_ref, lw_ref = take(6)
    states = dict((c, take(1)[0]) for c in ending)
    owns = dict((c, take(1)[0]) for c in ending)
    sources = dict((c, take(3)) for c in ending)
    if last:
        (rank_ref,) = take(1)
        final_ref, energy_ref = take(2)
        news = None
    else:
        kept = dict((c, take(1)[0]) for c in range(3) if c not in ending)
        before = take(3) if n % 2 == 1 else None
        half_sums = take(3) if n == 3 else None
        req_ref, send_blk_ref, send_lane_ref = take(3)
        news = dict((c, take(1)[0]) for c in ending)
        new_owns = dict((c, take(1)[0]) for c in ending)
        new_traces = dict((c, take(2**c)) for c in ending)
        sums = take(3) if n % 2 == 1 else None
        full_sums = take(3) if n == 3 else None
        out_a_ref, out_b_ref = take(2)
    ghost_ref, stack_ref, moved_ref, chosen_ref, cstack_ref, near_ref, flux_ref, fstack_ref = take(8)
    if last:
        (new_scratch,) = take(1)
        news = dict((c, new_scratch.at[c]) for c in range(3))
    else:
        d_ref, msg_ref = take(2)
    for at, c in enumerate(ending):
        unpack(dev_ref, at, got_a, got_b, ghost_ref)
        correct(
            states[c], owns[c], sources[c], ghost_ref, code_ref, lane_ref, orient_ref, c,
            star_ref.at[c], fl_ref.at[c], fn_ref.at[c], w_ref, ow_ref, lw_ref,
            stack_ref, moved_ref, chosen_ref, cstack_ref, near_ref, flux_ref, fstack_ref, news[c],
        )
    if last:
        total = jnp.zeros((8, L), F32)
        for c in range(3):
            for q in range(Q):
                v = news[c][q]
                total = total + jnp.sum((v * v).reshape(B // 8, 8, L), axis=0)
        line = jnp.sum(total, axis=0, keepdims=True)
        energy_ref[...] = jnp.broadcast_to(line[None], energy_ref.shape)
        for b in range(3):
            blk = rows_of(rank_ref[0:1, class_lanes(b)], B)
            index = rows_of(rank_ref[1:2, class_lanes(b)], B)

            def unsort(q, carry):
                final_ref[q, :, class_lanes(b)] = pick([news[c][q] for c in range(3)], blk, index)
                return carry

            lax.fori_loop(0, Q, unsort, 0)
        return
    for c in ending:
        for q in range(Q):
            d_ref[0, q] = news[c][q]
        run_steps(ORDER - 1, star_ref.at[c], d_ref, w_ref, stack_ref, moved_ref)
        after_steps(c, d_ref, w_ref, stack_ref, new_owns[c], new_traces[c])
    now = [new_traces[c][0] if c in ending else kept[c] for c in range(3)]
    if sums is not None:
        for b in range(3):
            for q in range(Q):
                value = before[b][q] + now[b][q]
                sums[b][q] = value
                if full_sums is not None:
                    full_sums[b][q] = value + half_sums[b][q]
    given = {0: now, 1: sums, 2: full_sums}
    pack(
        dev_ref, [(g, given[g]) for g in sending], req_ref, send_blk_ref, send_lane_ref,
        chosen_ref, msg_ref, out_a_ref, out_b_ref,
    )


FIELD = (Q, B, L)
TRACE = (Q, 4 * FP, L)


def shards(
    state, class_label, stiffness, star, face_proj, orient_map, flux_local, flux_neigh,
    neighbor, neighbor_face, orientation, send_list,
):
    elements = state.shape[2]
    devices = lax.axis_size("dom")
    aligned = [[GROUP * k + i for i in range(GROUP)] for k in range(devices // GROUP)]
    shifted = [[(m + REACH) % devices for m in group] for group in aligned]

    def exchange(first, second):
        got_a = lax.all_to_all(first, "dom", 0, 0, axis_index_groups=aligned, tiled=True)
        got_b = lax.all_to_all(second, "dom", 0, 0, axis_index_groups=shifted, tiled=True)
        return got_a, got_b

    dev = lax.axis_index("dom").astype(I32).reshape(1)
    send = send_list.reshape(2, 4, 3, SLOTS).transpose(2, 0, 1, 3).reshape(6, L)
    send = jnp.concatenate([send, send[:2]], axis=0)
    smem = pl.BlockSpec(memory_space=pltpu.SMEM)
    whole = pl.BlockSpec(memory_space=pltpu.VMEM)

    def run(kernel, args, outs, scratch, name, with_dev=True):
        return pl.pallas_call(
            kernel,
            in_specs=[smem if with_dev and i == 0 else whole for i in range(len(args))],
            out_specs=[whole] * len(outs),
            out_shape=outs,
            scratch_shapes=scratch,
            compiler_params=pltpu.CompilerParams(vmem_limit_bytes=VMEM_LIMIT),
            name=name,
        )(*args)

    (order, rank, code, lane, orient, send_blk, send_lane, req_a, req_b, w, ow, lw) = run(
        index_kernel,
        [dev, class_label.reshape(1, elements), neighbor, neighbor_face, orientation, send, stiffness, face_proj, orient_map],
        [shape((8, elements), I32)] * 2 + [shape((3, 8, L), I32)] * 3 + [shape((8, L), I32)] * 2
        + [shape((GROUP, 8, L), I32)] * 2
        + [shape((WROWS, 192), BF16), shape((3 * FP, 96), BF16), shape((288, B), BF16)],
        [pltpu.VMEM((WROWS, 192), F32), pltpu.VMEM((3 * FP, 96), F32), pltpu.VMEM((288, B), F32)],
        "index",
    )
    got_req = exchange(req_a, req_b)
    stack = pltpu.VMEM((192, Q * L), BF16)
    moved = pltpu.VMEM((Q, WROWS, L), F32)
    (sorted_state, star_s, fl_s, fn_s, own0, own1, own2, t00, t10, t11, t20, t21, t22, t23) = run(
        first_kernel,
        [state, star, flux_local, flux_neigh, order, w],
        [shape((3,) + FIELD), shape((3, 27, 16, L)), shape((3, 36, 16, L)), shape((3, 36, 16, L))]
        + [shape(FIELD)] * 3 + [shape(TRACE)] * 7,
        [pltpu.VMEM((3, ORDER) + FIELD, F32), stack, moved],
        "first",
        with_dev=False,
    )
    gat = pltpu.VMEM((Q, FP, L), F32)
    msg = pltpu.VMEM((PEERS, MSG, 8, L), F32)
    req, out_a, out_b = run(
        first_pack_kernel,
        [dev, *got_req, send_blk, send_lane, t00, t10, t20],
        [shape((8, L), I32)] + [shape((GROUP, 1, MSG, 8, L))] * 2,
        [gat, msg],
        "first_pack",
    )
    fields = [sorted_state[c] for c in range(3)]
    owns = [own0, own1, own2]
    later = {1: {0: t10, 1: t11}, 2: {0: t20, 1: t21, 2: t22, 3: t23}}
    now = [t00, t10, t20]
    sources = {0: now}
    half_sums = None
    for n in range(1, STEPS + 1):
        ending = [c for c in range(3) if n % 2**c == 0]
        got_a, got_b = exchange(out_a, out_b)
        args = [dev, got_a, got_b, code, lane, orient, star_s, fl_s, fn_s, w, ow, lw]
        args += [fields[c] for c in ending] + [owns[c] for c in ending]
        for c in ending:
            args += sources[c]
        common = [
            pltpu.VMEM((2, Q, FP, L), F32), stack, moved, gat, pltpu.VMEM((96, Q * L), BF16),
            pltpu.VMEM(TRACE, F32), pltpu.VMEM(TRACE, F32), pltpu.VMEM((288, Q * L), BF16),
        ]

        def kernel(*refs, n=n):
            step_kernel(n, *refs)

        if n == STEPS:
            final_state, energy_out = run(
                kernel,
                args + [rank],
                [shape((Q, B, elements)), shape((devices, 1, L))],
                common + [pltpu.VMEM((3,) + FIELD, F32)],
                "last",
            )
            break
        sending = [c for c in range(3) if (n + 1) % 2**c == 0]
        kept = [c for c in range(3) if c not in ending]
        args += [later[c][n % 2**c] for c in kept]
        if n % 2 == 1:
            args += now
        if n == 3:
            args += half_sums
        args += [req, send_blk, send_lane]
        outs = [shape(FIELD)] * (2 * len(ending)) + [shape(TRACE)] * sum(2**c for c in ending)
        outs += [shape(TRACE)] * (3 if n % 2 == 1 else 0) + [shape(TRACE)] * (3 if n == 3 else 0)
        outs += [shape((GROUP, len(sending), MSG, 8, L))] * 2
        got = list(run(kernel, args, outs, common + [pltpu.VMEM((ORDER,) + FIELD, F32), msg], "step%d" % n))
        for c in ending:
            fields[c] = got.pop(0)
        for c in ending:
            owns[c] = got.pop(0)
        for c in ending:
            made = [got.pop(0) for _ in range(2**c)]
            later[c] = dict(enumerate(made))
        now = [later[c][n % 2**c] for c in range(3)]
        sources = {0: now}
        if n % 2 == 1:
            sums = [got.pop(0) for _ in range(3)]
            sources[1] = sums
            if n == 1:
                half_sums = sums
        if n == 3:
            sources[2] = [got.pop(0) for _ in range(3)]
        out_a, out_b = got
    spread = lax.all_to_all(energy_out, "dom", 0, 0, tiled=True)
    energy = jnp.sum(spread).reshape(1) / (devices * elements * Q * B)
    return final_state, energy


def solution(mesh):
    in_specs = (
        P(None, None, "dom"),
        P("dom"),
        P(),
        P(None, None, None, "dom"),
        P(),
        P(),
        P(None, None, None, "dom"),
        P(None, None, None, "dom"),
        P(None, "dom"),
        P(None, "dom"),
        P(None, "dom"),
        P("dom", None),
    )
    out_specs = (P(None, None, "dom"), P())
    return jax.shard_map(shards, mesh=mesh, in_specs=in_specs, out_specs=out_specs, check_vma=False)
```

```python
import math

import jax
import jax.numpy as jnp
from jax import lax
from jax.experimental import pallas as pl
from jax.experimental.pallas import tpu as pltpu
from jax.sharding import PartitionSpec as P

ORDER = 6
Q = 9
B = 56
FB = 21
FP = 24
L = 128
REACH = 4
PEERS = 8
SLOTS = 32
GROUP = 8
STEPS = 4
OFFSETS = [p - REACH if p < REACH else p - REACH + 1 for p in range(PEERS)]
KROWS = 3 * B
WROWS = KROWS + 4 * FP
MSG = 7
HALF = 224
TROWS = Q * FP
SOURCES = 12
NEIGH = 4
STAR = 8
F32 = jnp.float32
BF16 = jnp.bfloat16
I32 = jnp.int32
VMEM_LIMIT = 40 * 1024 * 1024


def shape(dims, dtype=F32):
    return jax.ShapeDtypeStruct(dims, dtype)


def lane_take(x, index):
    numbers = lax.GatherDimensionNumbers(
        offset_dims=(),
        collapsed_slice_dims=(1,),
        start_index_map=(1,),
        operand_batching_dims=(0,),
        start_indices_batching_dims=(0,),
    )
    return lax.gather(
        x,
        index[..., None],
        numbers,
        slice_sizes=(1, 1),
        mode=lax.GatherScatterMode.PROMISE_IN_BOUNDS,
    )


def pick(blocks, code, lane):
    out = lane_take(blocks[0], lane)
    for k in range(1, len(blocks)):
        out = jnp.where(code == k, lane_take(blocks[k], lane), out)
    return out


def rows_of(vec, rows):
    return jnp.broadcast_to(vec, (rows, L))


def split(values):
    hi = values.astype(BF16)
    lo = (values - hi.astype(F32)).astype(BF16)
    return hi, lo


def put_stack(ref, q, values, rows):
    have = values.shape[0]
    if have < rows:
        values = jnp.concatenate([values, jnp.zeros((rows - have, L), F32)], axis=0)
    hi, lo = split(values)
    cols = slice(q * L, (q + 1) * L)
    ref[0:rows, cols] = hi
    ref[rows : 2 * rows, cols] = lo
    ref[2 * rows : 3 * rows, cols] = hi


def column_tiles():
    return [(t, min(2, Q - t)) for t in range(0, Q, 2)]


def product(weights, stack_ref, store, contract=1):
    for start, count in column_tiles():
        cols = slice(start * L, (start + count) * L)
        out = lax.dot_general(
            weights,
            stack_ref[:, cols],
            (((contract,), (0,)), ((), ())),
            preferred_element_type=F32,
        )
        for j in range(count):
            store(start + j, out[:, j * L : (j + 1) * L])


def mix_groups(total, most):
    groups = []
    at = 0
    while at < total:
        size = min(most, total - at)
        groups.append((at, size))
        at += size
    return groups


def row_bcast(ref, at, row):
    return jnp.broadcast_to(ref[at, pl.ds(row, 1), :], (8, L))[None]


def star_mix(mats_ref, moved_ref, put):
    for r0, rn in mix_groups(B, 32):
        acc = [None] * Q
        for d in range(3):
            for q in range(Q):
                m = moved_ref[q, d * B + r0 : d * B + r0 + rn, :].reshape(rn // 8, 8, L)
                for p in range(Q):
                    term = row_bcast(mats_ref, p * Q + q, STAR + d) * m
                    acc[p] = term if acc[p] is None else acc[p] + term
        for p in range(Q):
            put(p, r0, rn, acc[p].reshape(rn, L))


def class_lanes(c):
    return slice(c * L, (c + 1) * L)


def nt_dot(a, b):
    return lax.dot_general(a, b, (((1,), (1,)), ((), ())), preferred_element_type=F32)


def index_kernel(
    dev_ref, label_ref, nbr_ref, face_ref, orient_ref, send_ref, stiff_ref, proj_ref, omap_ref,
    order_ref, rank_ref, near_ref, sorted_orient_ref, send_ref_out,
    req_a_ref, req_b_ref, w_ref, ow_ref, lw_ref,
    wf_ref, owf_ref, lwf_ref,
):
    n_el = label_ref.shape[1]
    wf_ref[...] = jnp.zeros_like(wf_ref)
    owf_ref[...] = jnp.zeros_like(owf_ref)
    for d in range(3):
        k = stiff_ref[d]
        hi = k.astype(BF16).astype(F32)
        rows = slice(d * B, (d + 1) * B)
        wf_ref[rows, 0:B] = hi
        wf_ref[rows, 64 : 64 + B] = hi
        wf_ref[rows, 128 : 128 + B] = k - hi
    lwf_ref[...] = jnp.zeros_like(lwf_ref)
    for j in range(4):
        k = proj_ref[j]
        hi = k.astype(BF16).astype(F32)
        rows = slice(KROWS + j * FP, KROWS + j * FP + FB)
        wf_ref[rows, 0:B] = hi
        wf_ref[rows, 64 : 64 + B] = hi
        wf_ref[rows, 128 : 128 + B] = k - hi
        lwf_ref[j * FP : j * FP + FB, :] = hi
        lwf_ref[96 + j * FP : 96 + j * FP + FB, :] = hi
        lwf_ref[192 + j * FP : 192 + j * FP + FB, :] = k - hi
    for h in range(3):
        k = omap_ref[h]
        hi = k.astype(BF16).astype(F32)
        rows = slice(h * FP, h * FP + FB)
        owf_ref[rows, 0:FB] = hi
        owf_ref[rows, 32 : 32 + FB] = hi
        owf_ref[rows, 64 : 64 + FB] = k - hi
    w_ref[...] = wf_ref[...].astype(BF16)
    ow_ref[...] = owf_ref[...].astype(BF16)
    lw_ref[...] = lwf_ref[...].astype(BF16)
    label = label_ref[...]
    classes = lax.broadcasted_iota(I32, (8, n_el), 0)
    hot = (jnp.broadcast_to(label, (8, n_el)) == classes).astype(F32)
    row = lax.broadcasted_iota(I32, (n_el, n_el), 0)
    col = lax.broadcasted_iota(I32, (n_el, n_el), 1)
    before = (row < col).astype(F32).astype(BF16)
    prefix = jnp.dot(hot.astype(BF16), before, preferred_element_type=F32)
    base = classes.astype(F32) * float(L)
    rank = jnp.sum(hot * (prefix + base), axis=0, keepdims=True).astype(I32)
    here = (jnp.broadcast_to(rank, (n_el, n_el)) == row).astype(F32).astype(BF16)
    ids = lax.broadcasted_iota(I32, (8, n_el), 1)
    first = lax.broadcasted_iota(I32, (8, n_el), 0) == 0
    parts = jnp.where(first, ids // L, ids % L).astype(F32).astype(BF16)
    order = nt_dot(parts, here).astype(I32)
    order_ref[...] = order
    rank_ref[...] = jnp.where(first, jnp.broadcast_to(rank >> 7, (8, n_el)), jnp.broadcast_to(rank & 127, (8, n_el)))
    rank_blocks = [rows_of(rank[:, class_lanes(c)], 8) for c in range(3)]
    pad = jnp.zeros((4, n_el), I32)
    tables = [jnp.concatenate([ref[...], pad], axis=0) for ref in (nbr_ref, face_ref, orient_ref)]
    sub = lax.broadcasted_iota(I32, (8, L), 0)
    lanes = lax.broadcasted_iota(I32, (8, L), 1)
    for c in range(3):
        blk = rows_of(order[0:1, class_lanes(c)], 8)
        lane = rows_of(order[1:2, class_lanes(c)], 8)
        nbr, face, orient = [
            pick([t[:, class_lanes(b)] for b in range(3)], blk, lane) for t in tables
        ]
        ghost = nbr >= n_el
        inside = jnp.where(ghost, 0, nbr)
        place = pick(rank_blocks, inside >> 7, inside & 127)
        slot = jnp.where(ghost, nbr - n_el, 0)
        peer = ((slot >> 5) * 11) >> 5
        slot = peer * SLOTS + (slot & 31)
        near_ref[c] = jnp.where(ghost, SOURCES * L + slot, face * (3 * L) + place)
        sorted_orient_ref[c] = orient
        slot = jnp.where(ghost, slot, -1)
        want = jnp.zeros((8, 2 * L), F32)
        target = lax.broadcasted_iota(I32, (2 * L, L), 0)
        for f in range(4):
            match = (jnp.broadcast_to(slot[f : f + 1], (2 * L, L)) == target).astype(F32).astype(BF16)
            value = rows_of(face[f : f + 1], 8).astype(F32).astype(BF16)
            want = want + nt_dot(value, match)
        want = want.astype(I32)
        for p in range(PEERS):
            half = want[:, class_lanes(p // 4)]
            turn = (-(p % 4) * SLOTS) % L
            moved = pltpu.roll(half, turn, axis=1) if turn else half
            wf_ref[8 * p : 8 * p + 8, 0:L] = jnp.where(
                sub == c, moved.astype(F32), wf_ref[8 * p : 8 * p + 8, 0:L]
            )
    place_in_group = dev_ref[0] % GROUP
    other_place = (place_in_group + REACH) % GROUP
    for p in range(PEERS):
        message = wf_ref[8 * p : 8 * p + 8, 0:L].astype(I32)
        to = place_in_group + OFFSETS[p]
        within = jnp.logical_and(to >= 0, to < GROUP)

        @pl.when(within)
        def _():
            req_a_ref[jnp.where(within, to, 0)] = message

        @pl.when(jnp.logical_not(within))
        def _():
            req_b_ref[jnp.where(within, 0, other_place + OFFSETS[p])] = message

    send = jnp.maximum(send_ref[...], 0)
    place = pick(rank_blocks, send >> 7, send & 127)
    send_ref_out[...] = place


def run_steps(count, mats_ref, d_ref, w_ref, stack_ref, moved_ref):
    def body(k, carry):
        for q in range(Q):
            put_stack(stack_ref, q, d_ref[k, q], 64)

        def store(q, out):
            moved_ref[q, 0:KROWS] = out

        product(w_ref[0:KROWS, :], stack_ref, store)

        def put(p, r0, rn, value):
            d_ref[k + 1, p, r0 : r0 + rn, :] = value

        star_mix(mats_ref, moved_ref, put)
        return carry

    lax.fori_loop(0, count, body, 0)


def weights_between(start, end):
    return [(float(end) ** (k + 1) - float(start) ** (k + 1)) / math.factorial(k + 1) for k in range(ORDER)]


def integrate(d_ref, q, start, end):
    total = None
    for k, weight in enumerate(weights_between(start, end)):
        term = d_ref[k, q] * weight
        total = term if total is None else total + term
    return total


def traces(d_ref, w_ref, stack_ref, start, trace_ref):
    for q in range(Q):
        put_stack(stack_ref, q, integrate(d_ref, q, start, start + 1), 64)

    def store(q, out):
        trace_ref[q] = out

    product(w_ref[KROWS:WROWS, :], stack_ref, store)


def after_steps(c, d_ref, w_ref, stack_ref, own_ref, trace_refs):
    span = 2**c
    for t in range(span):
        traces(d_ref, w_ref, stack_ref, t, trace_refs[t])
    for q in range(Q):
        own_ref[q] = integrate(d_ref, q, 0, span)


def block_transpose(four, lane):
    a, b, c, d = four
    low = (lane & 64) == 0
    a, c = jnp.where(low, a, pltpu.roll(c, 64, axis=1)), jnp.where(low, pltpu.roll(a, 64, axis=1), c)
    b, d = jnp.where(low, b, pltpu.roll(d, 64, axis=1)), jnp.where(low, pltpu.roll(b, 64, axis=1), d)
    low = (lane & 32) == 0
    a, b = jnp.where(low, a, pltpu.roll(b, 32, axis=1)), jnp.where(low, pltpu.roll(a, 96, axis=1), b)
    c, d = jnp.where(low, c, pltpu.roll(d, 32, axis=1)), jnp.where(low, pltpu.roll(c, 96, axis=1), d)
    return [a, b, c, d]


def one_hot(hot_ref, index_ref, at, count, rows):
    for f in range(count):
        index = index_ref[at + f : at + f + 1, :]
        for k in range(0, rows, 2 * L):
            row = lax.broadcasted_iota(I32, (2 * L, L), 0) + k
            match = jnp.broadcast_to(index, (2 * L, L)) == row
            hot_ref[k : k + 2 * L, f * L : (f + 1) * L] = match.astype(F32).astype(BF16)


def stack_rows(ref, at, column, values):
    hi, lo = split(values)
    rows = values.shape[0]
    cols = slice(column * L, (column + 1) * L)
    ref[at : at + rows, cols] = hi
    ref[HALF + at : HALF + at + rows, cols] = lo


def stack_traces(lhs_ref, sources):
    for b in range(3):
        for j in range(4):
            rows = slice(j * FP, (j + 1) * FP)
            for q in range(0, Q - 1, 2):
                two = jnp.concatenate([sources[b][q, rows, :], sources[b][q + 1, rows, :]], axis=0)
                stack_rows(lhs_ref, q * FP, j * 3 + b, two)
            stack_rows(lhs_ref, (Q - 1) * FP, j * 3 + b, sources[b][Q - 1, rows, :])


def both(out):
    return out[0:TROWS] + out[HALF : HALF + TROWS]


def pack(dev_ref, rows, send_ref, hot_ref, gat_ref, msg_ref, out_a_ref, out_b_ref):
    place_in_group = dev_ref[0] % GROUP
    other_place = (place_in_group + REACH) % GROUP
    lane = lax.broadcasted_iota(I32, (8, L), 1)
    for at, (g, lhs_ref) in enumerate(rows):
        one_hot(hot_ref, send_ref, 2 * g, 2, SOURCES * L)
        out = jnp.dot(lhs_ref[...], hot_ref[0 : SOURCES * L, 0 : 2 * L], preferred_element_type=F32)
        gat_ref[:, 0 : 2 * L] = both(out)
        for half in range(2):
            for v in range(MSG):
                four = []
                for k in range(4):
                    t = MSG * k + v
                    if t < 3 * Q:
                        four.append(gat_ref[8 * t : 8 * t + 8, class_lanes(half)])
                    else:
                        four.append(jnp.zeros((8, L), F32))
                for k, value in enumerate(block_transpose(four, lane)):
                    msg_ref[4 * half + k, v] = value
        for p in range(PEERS):
            to = place_in_group + OFFSETS[p]
            within = jnp.logical_and(to >= 0, to < GROUP)

            @pl.when(within)
            def _():
                out_a_ref[jnp.where(within, to, 0), at] = msg_ref[p]

            @pl.when(jnp.logical_not(within))
            def _():
                out_b_ref[jnp.where(within, 0, other_place + OFFSETS[p]), at] = msg_ref[p]


def unpack(dev_ref, at, got_a_ref, got_b_ref, gat_ref, ghost_ref):
    place_in_group = dev_ref[0] % GROUP
    other_place = (place_in_group + REACH) % GROUP
    lane = lax.broadcasted_iota(I32, (8, L), 1)
    for half in range(2):
        found = []
        for k in range(4):
            at_group = place_in_group + OFFSETS[4 * half + k]
            within = jnp.logical_and(at_group >= 0, at_group < GROUP)
            first = got_a_ref[jnp.where(within, at_group, 0), at]
            second = got_b_ref[jnp.where(within, 0, other_place + OFFSETS[4 * half + k]), at]
            found.append(jnp.where(within, first, second))
        for v in range(MSG):
            moved = block_transpose([found[k][v] for k in range(4)], lane)
            for k in range(4):
                t = MSG * k + v
                if t < 3 * Q:
                    gat_ref[8 * t : 8 * t + 8, class_lanes(half)] = moved[k]
        stack_rows(ghost_ref, 0, half, gat_ref[:, class_lanes(half)])


def correct(
    state_ref, own_ref, lhs_ref, ghost_ref, index_ref, orient_ref, mats_ref, w_ref, ow_ref, lw_ref,
    stack_ref, moved_ref, hot_ref, gat_ref, cstack_ref, near_ref, flux_ref, fstack_ref, new_ref,
):
    for q in range(Q):
        put_stack(stack_ref, q, own_ref[q], 64)

    def store(q, out):
        moved_ref[q] = out

    product(w_ref[...], stack_ref, store)

    def put(p, r0, rn, value):
        new_ref[p, r0 : r0 + rn, :] = state_ref[p, r0 : r0 + rn, :] + value

    star_mix(mats_ref, moved_ref, put)
    one_hot(hot_ref, index_ref, 0, 4, (SOURCES + 2) * L)
    out = jnp.dot(lhs_ref[...], hot_ref[0 : SOURCES * L, :], preferred_element_type=F32)
    out = out + jnp.dot(ghost_ref[...], hot_ref[SOURCES * L :, :], preferred_element_type=F32)
    gat_ref[...] = both(out)
    for f in range(4):
        for q in range(Q):
            put_stack(cstack_ref, q, gat_ref[q * FP : (q + 1) * FP, f * L : (f + 1) * L], 32)
        turn = rows_of(orient_ref[f : f + 1, :], FP)

        def store_near(q, out):
            value = jnp.where(turn == 1, out[FP : 2 * FP], out[0:FP])
            near_ref[q, f * FP : (f + 1) * FP] = jnp.where(turn == 2, out[2 * FP :], value)

        product(ow_ref[...], cstack_ref, store_near)

    def flux_body(f, carry):
        acc = [None] * Q
        r = pl.multiple_of(f * FP, 8)
        for q in range(Q):
            mine = moved_ref[q, pl.ds(KROWS + r, FP), :].reshape(3, 8, L)
            theirs = near_ref[q, pl.ds(r, FP), :].reshape(3, 8, L)
            for p in range(Q):
                term = row_bcast(mats_ref, p * Q + q, f) * mine
                acc[p] = term if acc[p] is None else acc[p] + term
                acc[p] = acc[p] + row_bcast(mats_ref, p * Q + q, NEIGH + f) * theirs
        for p in range(Q):
            flux_ref[p, pl.ds(r, FP), :] = acc[p].reshape(FP, L)
        return carry

    lax.fori_loop(0, 4, flux_body, 0)
    for p in range(Q):
        put_stack(fstack_ref, p, flux_ref[p], 96)

    def subtract(p, out):
        new_ref[p] = new_ref[p] - out

    product(lw_ref[...], fstack_ref, subtract, contract=0)


def read_requests(dev_ref, req_a_ref, req_b_ref, place_ref, send_ref):
    place_in_group = dev_ref[0] % GROUP
    other_place = (place_in_group + REACH) % GROUP
    lane = lax.broadcasted_iota(I32, (1, L), 1)
    rows = [jnp.zeros((1, L), I32) for _ in range(6)]
    for p in range(PEERS):
        at_group = place_in_group + OFFSETS[p]
        within = jnp.logical_and(at_group >= 0, at_group < GROUP)
        first = req_a_ref[jnp.where(within, at_group, 0)]
        second = req_b_ref[jnp.where(within, 0, other_place + OFFSETS[p])]
        message = jnp.where(within, first, second)
        turn = (p % 4) * SLOTS
        message = pltpu.roll(message, turn, axis=1) if turn else message
        part = (lane >> 5) == (p % 4)
        for g in range(3):
            row = 2 * g + p // 4
            rows[row] = jnp.where(part, message[g : g + 1], rows[row])
    for row in range(8):
        send_ref[row : row + 1] = rows[row % 6] * (3 * L) + place_ref[row : row + 1]


def first_kernel(
    dev_ref, req_a_ref, req_b_ref, place_ref, state_ref, star_ref, fl_ref, fn_ref, order_ref, w_ref,
    s0, s1, s2, mats, own0, own1, own2, t00, t10, t11, t20, t21, t22, t23, send_ref, lhs_ref,
    out_a_ref, out_b_ref,
    d_ref, stack_ref, moved_ref, hot_ref, gat_ref, msg_ref,
):
    picks = []
    for c in range(3):
        picks.append((order_ref[0:1, class_lanes(c)], order_ref[1:2, class_lanes(c)]))
    states = [s0, s1, s2]

    def sort_rows(blocks, put):
        rows = blocks[0].shape[0]
        for c in range(3):
            put(c, pick(blocks, rows_of(picks[c][0], rows), rows_of(picks[c][1], rows)))

    def sort_state(q, carry):
        def put(c, value):
            states[c][q] = value
            d_ref[c, 0, q] = value

        sort_rows([state_ref[q, :, class_lanes(b)] for b in range(3)], put)
        return carry

    lax.fori_loop(0, Q, sort_state, 0)

    def sort_matrices(p, carry):
        for q in range(Q):
            at = p * Q + q

            def put_flux(c, value):
                mats[c, at, 0:8, :] = value

            def put_star(c, value):
                mats[c, at, STAR : STAR + 3, :] = value

            sort_rows(
                [
                    jnp.concatenate([fl_ref[p, q, :, class_lanes(b)], fn_ref[p, q, :, class_lanes(b)]], axis=0)
                    for b in range(3)
                ],
                put_flux,
            )
            sort_rows([star_ref[p, q, :, class_lanes(b)] for b in range(3)], put_star)
        return carry

    lax.fori_loop(0, Q, sort_matrices, 0)

    def each(c, carry):
        run_steps(ORDER - 1, mats.at[c], d_ref.at[c], w_ref, stack_ref, moved_ref)
        return carry

    lax.fori_loop(0, 3, each, 0)
    after_steps(0, d_ref.at[0], w_ref, stack_ref, own0, [t00])
    after_steps(1, d_ref.at[1], w_ref, stack_ref, own1, [t10, t11])
    after_steps(2, d_ref.at[2], w_ref, stack_ref, own2, [t20, t21, t22, t23])
    read_requests(dev_ref, req_a_ref, req_b_ref, place_ref, send_ref)
    stack_traces(lhs_ref, [t00, t10, t20])
    pack(dev_ref, [(0, lhs_ref)], send_ref, hot_ref, gat_ref, msg_ref, out_a_ref, out_b_ref)


def step_kernel(n, *refs):
    refs = list(refs)

    def take(count):
        got = refs[:count]
        del refs[:count]
        return got

    ending = [c for c in range(3) if n % 2**c == 0]
    sending = [c for c in range(3) if (n + 1) % 2**c == 0] if n < STEPS else []
    last = n == STEPS
    (dev_ref, got_a, got_b, index_ref, orient_ref) = take(5)
    (mats,) = take(1)
    w_ref, ow_ref, lw_ref = take(3)
    states = dict((c, take(1)[0]) for c in ending)
    owns = dict((c, take(1)[0]) for c in ending)
    sources = dict((c, take(1)[0]) for c in ending)
    if last:
        (rank_ref,) = take(1)
        final_ref, energy_ref = take(2)
        news = None
    else:
        kept = dict((c, take(1)[0]) for c in range(3) if c not in ending)
        before = take(3) if n % 2 == 1 else None
        half_sums = take(3) if n == 3 else None
        (send_ref,) = take(1)
        news = dict((c, take(1)[0]) for c in ending)
        new_owns = dict((c, take(1)[0]) for c in ending)
        new_traces = dict((c, take(2**c)) for c in ending)
        sums = take(3) if n == 1 else None
        lhs = dict((c, take(1)[0]) for c in sending)
        out_a_ref, out_b_ref = take(2)
    ghost_ref, stack_ref, moved_ref, hot_ref, gat_ref, cstack_ref, near_ref, flux_ref, fstack_ref = take(9)
    if last:
        (new_scratch,) = take(1)
        news = dict((c, new_scratch.at[c]) for c in range(3))
    else:
        d_ref, msg_ref = take(2)
        if n == 3:
            sums = take(3)
    for at, c in enumerate(ending):
        unpack(dev_ref, at, got_a, got_b, gat_ref, ghost_ref)
        correct(
            states[c], owns[c], sources[c], ghost_ref, index_ref.at[c], orient_ref.at[c],
            mats.at[c], w_ref, ow_ref, lw_ref,
            stack_ref, moved_ref, hot_ref, gat_ref, cstack_ref, near_ref, flux_ref, fstack_ref, news[c],
        )
    if last:
        total = jnp.zeros((8, L), F32)
        for c in range(3):
            for q in range(Q):
                v = news[c][q]
                total = total + jnp.sum((v * v).reshape(B // 8, 8, L), axis=0)
        line = jnp.sum(total, axis=0, keepdims=True)
        energy_ref[...] = jnp.broadcast_to(line[None], energy_ref.shape)
        for b in range(3):
            blk = rows_of(rank_ref[0:1, class_lanes(b)], B)
            index = rows_of(rank_ref[1:2, class_lanes(b)], B)

            def unsort(q, carry):
                final_ref[q, :, class_lanes(b)] = pick([news[c][q] for c in range(3)], blk, index)
                return carry

            lax.fori_loop(0, Q, unsort, 0)
        return
    for c in ending:
        for q in range(Q):
            d_ref[0, q] = news[c][q]
        run_steps(ORDER - 1, mats.at[c], d_ref, w_ref, stack_ref, moved_ref)
        after_steps(c, d_ref, w_ref, stack_ref, new_owns[c], new_traces[c])
    now = [new_traces[c][0] if c in ending else kept[c] for c in range(3)]
    stack_traces(lhs[0], now)
    if sums is not None:
        for b in range(3):
            for q in range(Q):
                sums[b][q] = before[b][q] + now[b][q]
        stack_traces(lhs[1], sums)
    if n == 3:
        for b in range(3):
            for q in range(Q):
                sums[b][q] = sums[b][q] + half_sums[b][q]
        stack_traces(lhs[2], sums)
    pack(dev_ref, [(g, lhs[g]) for g in sending], send_ref, hot_ref, gat_ref, msg_ref, out_a_ref, out_b_ref)


FIELD = (Q, B, L)
TRACE = (Q, 4 * FP, L)


def shards(
    state, class_label, stiffness, star, face_proj, orient_map, flux_local, flux_neigh,
    neighbor, neighbor_face, orientation, send_list,
):
    elements = state.shape[2]
    devices = lax.axis_size("dom")
    aligned = [[GROUP * k + i for i in range(GROUP)] for k in range(devices // GROUP)]
    shifted = [[(m + REACH) % devices for m in group] for group in aligned]

    def exchange(first, second):
        got_a = lax.all_to_all(first, "dom", 0, 0, axis_index_groups=aligned, tiled=True)
        got_b = lax.all_to_all(second, "dom", 0, 0, axis_index_groups=shifted, tiled=True)
        return got_a, got_b

    dev = lax.axis_index("dom").astype(I32).reshape(1)
    send = send_list.reshape(2, 4, 3, SLOTS).transpose(2, 0, 1, 3).reshape(6, L)
    send = jnp.concatenate([send, send[:2]], axis=0)
    smem = pl.BlockSpec(memory_space=pltpu.SMEM)
    whole = pl.BlockSpec(memory_space=pltpu.VMEM)

    def run(kernel, args, outs, scratch, name, with_dev=True):
        return pl.pallas_call(
            kernel,
            in_specs=[smem if with_dev and i == 0 else whole for i in range(len(args))],
            out_specs=[whole] * len(outs),
            out_shape=outs,
            scratch_shapes=scratch,
            compiler_params=pltpu.CompilerParams(vmem_limit_bytes=VMEM_LIMIT),
            name=name,
        )(*args)

    (order, rank, near, orient, place, req_a, req_b, w, ow, lw) = run(
        index_kernel,
        [dev, class_label.reshape(1, elements), neighbor, neighbor_face, orientation, send, stiffness, face_proj, orient_map],
        [shape((8, elements), I32)] * 2 + [shape((3, 8, L), I32)] * 2 + [shape((8, L), I32)]
        + [shape((GROUP, 8, L), I32)] * 2
        + [shape((WROWS, 192), BF16), shape((3 * FP, 96), BF16), shape((288, B), BF16)],
        [pltpu.VMEM((WROWS, 192), F32), pltpu.VMEM((3 * FP, 96), F32), pltpu.VMEM((288, B), F32)],
        "index",
    )
    got_req = exchange(req_a, req_b)
    stack = pltpu.VMEM((192, Q * L), BF16)
    moved = pltpu.VMEM((Q, WROWS, L), F32)
    hot = pltpu.VMEM(((SOURCES + 2) * L, 4 * L), BF16)
    gat = pltpu.VMEM((TROWS, 4 * L), F32)
    msg = pltpu.VMEM((PEERS, MSG, 8, L), F32)
    stacked = shape((2 * HALF, SOURCES * L), BF16)

    def matrices(array):
        return array.transpose(1, 2, 0, 3)

    got = list(
        run(
            first_kernel,
            [dev, *got_req, place, state, matrices(star), matrices(flux_local), matrices(flux_neigh), order, w],
            [shape(FIELD)] * 3 + [shape((3, Q * Q, 16, L))] + [shape(FIELD)] * 3 + [shape(TRACE)] * 7
            + [shape((8, L), I32), stacked] + [shape((GROUP, 1, MSG, 8, L))] * 2,
            [pltpu.VMEM((3, ORDER) + FIELD, F32), stack, moved, hot, gat, msg],
            "first",
        )
    )
    fields = got[0:3]
    mats = got[3]
    owns = got[4:7]
    t00, t10, t11, t20, t21, t22, t23, send_index, lhs, out_a, out_b = got[7:]
    later = {1: {0: t10, 1: t11}, 2: {0: t20, 1: t21, 2: t22, 3: t23}}
    now = [t00, t10, t20]
    sources = {0: lhs}
    half_sums = None
    for n in range(1, STEPS + 1):
        ending = [c for c in range(3) if n % 2**c == 0]
        got_a, got_b = exchange(out_a, out_b)
        args = [dev, got_a, got_b, near, orient, mats, w, ow, lw]
        args += [fields[c] for c in ending] + [owns[c] for c in ending] + [sources[c] for c in ending]
        common = [
            pltpu.VMEM((2 * HALF, 2 * L), BF16), stack, moved, hot, gat, pltpu.VMEM((96, Q * L), BF16),
            pltpu.VMEM(TRACE, F32), pltpu.VMEM(TRACE, F32), pltpu.VMEM((288, Q * L), BF16),
        ]

        def kernel(*refs, n=n):
            step_kernel(n, *refs)

        if n == STEPS:
            final_state, energy_out = run(
                kernel,
                args + [rank],
                [shape((Q, B, elements)), shape((devices, 1, L))],
                common + [pltpu.VMEM((3,) + FIELD, F32)],
                "last",
            )
            break
        sending = [c for c in range(3) if (n + 1) % 2**c == 0]
        kept = [c for c in range(3) if c not in ending]
        args += [later[c][n % 2**c] for c in kept]
        if n % 2 == 1:
            args += now
        if n == 3:
            args += half_sums
        args += [send_index]
        outs = [shape(FIELD)] * (2 * len(ending)) + [shape(TRACE)] * sum(2**c for c in ending)
        outs += [shape(TRACE)] * (3 if n == 1 else 0) + [stacked] * len(sending)
        outs += [shape((GROUP, len(sending), MSG, 8, L))] * 2
        scratch = common + [pltpu.VMEM((ORDER,) + FIELD, F32), msg]
        scratch += [pltpu.VMEM(TRACE, F32)] * (3 if n == 3 else 0)
        got = list(run(kernel, args, outs, scratch, "step%d" % n))
        for c in ending:
            fields[c] = got.pop(0)
        for c in ending:
            owns[c] = got.pop(0)
        for c in ending:
            made = [got.pop(0) for _ in range(2**c)]
            later[c] = dict(enumerate(made))
        now = [later[c][n % 2**c] for c in range(3)]
        if n == 1:
            half_sums = [got.pop(0) for _ in range(3)]
        for c in sending:
            sources[c] = got.pop(0)
        out_a, out_b = got
    spread = lax.all_to_all(energy_out, "dom", 0, 0, tiled=True)
    energy = jnp.sum(spread).reshape(1) / (devices * elements * Q * B)
    return final_state, energy


def solution(mesh):
    in_specs = (
        P(None, None, "dom"),
        P("dom"),
        P(),
        P(None, None, None, "dom"),
        P(),
        P(),
        P(None, None, None, "dom"),
        P(None, None, None, "dom"),
        P(None, "dom"),
        P(None, "dom"),
        P(None, "dom"),
        P("dom", None),
    )
    out_specs = (P(None, None, "dom"), P())
    return jax.shard_map(shards, mesh=mesh, in_specs=in_specs, out_specs=out_specs, check_vma=False)
```

```python
import math

import jax
import jax.numpy as jnp
from jax import lax
from jax.experimental import pallas as pl
from jax.experimental.pallas import tpu as pltpu
from jax.sharding import PartitionSpec as P

ORDER = 6
Q = 9
B = 56
FB = 21
FP = 24
L = 128
REACH = 4
PEERS = 8
SLOTS = 32
GROUP = 8
STEPS = 4
OFFSETS = [p - REACH if p < REACH else p - REACH + 1 for p in range(PEERS)]
KROWS = 3 * B
WROWS = KROWS + 4 * FP
MSG = 7
HALF = 224
MSG0 = 16
HALF0 = 512
TILES = 3 * Q
TILES0 = 7 * Q
TROWS = Q * FP
SOURCES = 12
NEIGH = 4
STAR = 8
F32 = jnp.float32
BF16 = jnp.bfloat16
I32 = jnp.int32
VMEM_LIMIT = 40 * 1024 * 1024


def shape(dims, dtype=F32):
    return jax.ShapeDtypeStruct(dims, dtype)


def lane_take(x, index):
    numbers = lax.GatherDimensionNumbers(
        offset_dims=(),
        collapsed_slice_dims=(1,),
        start_index_map=(1,),
        operand_batching_dims=(0,),
        start_indices_batching_dims=(0,),
    )
    return lax.gather(
        x,
        index[..., None],
        numbers,
        slice_sizes=(1, 1),
        mode=lax.GatherScatterMode.PROMISE_IN_BOUNDS,
    )


def pick(blocks, code, lane):
    out = lane_take(blocks[0], lane)
    for k in range(1, len(blocks)):
        out = jnp.where(code == k, lane_take(blocks[k], lane), out)
    return out


def rows_of(vec, rows):
    return jnp.broadcast_to(vec, (rows, L))


def split(values):
    hi = values.astype(BF16)
    lo = (values - hi.astype(F32)).astype(BF16)
    return hi, lo


def put_stack(ref, q, values, rows):
    have = values.shape[0]
    if have < rows:
        values = jnp.concatenate([values, jnp.zeros((rows - have, L), F32)], axis=0)
    hi, lo = split(values)
    cols = slice(q * L, (q + 1) * L)
    ref[0:rows, cols] = hi
    ref[rows : 2 * rows, cols] = lo
    ref[2 * rows : 3 * rows, cols] = hi


def column_tiles():
    return [(t, min(2, Q - t)) for t in range(0, Q, 2)]


def product(weights, stack_ref, store, contract=1):
    for start, count in column_tiles():
        cols = slice(start * L, (start + count) * L)
        out = lax.dot_general(
            weights,
            stack_ref[:, cols],
            (((contract,), (0,)), ((), ())),
            preferred_element_type=F32,
        )
        for j in range(count):
            store(start + j, out[:, j * L : (j + 1) * L])


def mix_groups(total, most):
    groups = []
    at = 0
    while at < total:
        size = min(most, total - at)
        groups.append((at, size))
        at += size
    return groups


def row_bcast(ref, at, row):
    return jnp.broadcast_to(ref[at, pl.ds(row, 1), :], (8, L))[None]


def star_mix(mats_ref, moved_ref, put):
    for r0, rn in mix_groups(B, 32):
        acc = [None] * Q
        for d in range(3):
            for q in range(Q):
                m = moved_ref[q, d * B + r0 : d * B + r0 + rn, :].reshape(rn // 8, 8, L)
                for p in range(Q):
                    term = row_bcast(mats_ref, p * Q + q, STAR + d) * m
                    acc[p] = term if acc[p] is None else acc[p] + term
        for p in range(Q):
            put(p, r0, rn, acc[p].reshape(rn, L))


def class_lanes(c):
    return slice(c * L, (c + 1) * L)


def nt_dot(a, b):
    return lax.dot_general(a, b, (((1,), (1,)), ((), ())), preferred_element_type=F32)


def make_indices(
    label_ref, nbr_ref, face_ref, orient_ref, send_ref, stiff_ref, proj_ref, omap_ref,
    order_ref, rank_ref, near_ref, near_first_ref, sorted_orient_ref, place_ref, want_ref,
    w_ref, ow_ref, lw_ref, wf_ref, owf_ref, lwf_ref, pad_ref,
):
    n_el = nbr_ref.shape[1]
    wf_ref[...] = jnp.zeros_like(wf_ref)
    owf_ref[...] = jnp.zeros_like(owf_ref)
    for d in range(3):
        k = stiff_ref[d]
        hi = k.astype(BF16).astype(F32)
        rows = slice(d * B, (d + 1) * B)
        wf_ref[rows, 0:B] = hi
        wf_ref[rows, 64 : 64 + B] = hi
        wf_ref[rows, 128 : 128 + B] = k - hi
    lwf_ref[...] = jnp.zeros_like(lwf_ref)
    for j in range(4):
        k = proj_ref[:, j, :]
        hi = k.astype(BF16).astype(F32)
        rows = slice(KROWS + j * FP, KROWS + j * FP + FB)
        wf_ref[rows, 0:B] = hi
        wf_ref[rows, 64 : 64 + B] = hi
        wf_ref[rows, 128 : 128 + B] = k - hi
        lwf_ref[j * FP : j * FP + FB, :] = hi
        lwf_ref[96 + j * FP : 96 + j * FP + FB, :] = hi
        lwf_ref[192 + j * FP : 192 + j * FP + FB, :] = k - hi
    for h in range(3):
        k = omap_ref[h]
        hi = k.astype(BF16).astype(F32)
        rows = slice(h * FP, h * FP + FB)
        owf_ref[rows, 0:FB] = hi
        owf_ref[rows, 32 : 32 + FB] = hi
        owf_ref[rows, 64 : 64 + FB] = k - hi
    w_ref[...] = wf_ref[...].astype(BF16)
    ow_ref[...] = owf_ref[...].astype(BF16)
    lw_ref[...] = lwf_ref[...].astype(BF16)
    label = jnp.concatenate([label_ref[c : c + 1, :] for c in range(3)], axis=1)
    classes = lax.broadcasted_iota(I32, (8, n_el), 0)
    hot = (jnp.broadcast_to(label, (8, n_el)) == classes).astype(F32)
    row = lax.broadcasted_iota(I32, (n_el, n_el), 0)
    col = lax.broadcasted_iota(I32, (n_el, n_el), 1)
    before = (row < col).astype(F32).astype(BF16)
    prefix = jnp.dot(hot.astype(BF16), before, preferred_element_type=F32)
    base = classes.astype(F32) * float(L)
    rank = jnp.sum(hot * (prefix + base), axis=0, keepdims=True).astype(I32)
    here = (jnp.broadcast_to(rank, (n_el, n_el)) == row).astype(F32).astype(BF16)
    ids = lax.broadcasted_iota(I32, (8, n_el), 1)
    first = lax.broadcasted_iota(I32, (8, n_el), 0) == 0
    parts = jnp.where(first, ids // L, ids % L).astype(F32).astype(BF16)
    order = nt_dot(parts, here).astype(I32)
    order_ref[...] = order
    rank_ref[...] = jnp.where(first, jnp.broadcast_to(rank >> 7, (8, n_el)), jnp.broadcast_to(rank & 127, (8, n_el)))
    rank_blocks = [rows_of(rank[:, class_lanes(c)], 8) for c in range(3)]
    pad = jnp.zeros((4, n_el), I32)
    tables = [jnp.concatenate([ref[...], pad], axis=0) for ref in (nbr_ref, face_ref, orient_ref)]
    want_ref[...] = jnp.zeros_like(want_ref)
    for c in range(3):
        blk = rows_of(order[0:1, class_lanes(c)], 8)
        lane = rows_of(order[1:2, class_lanes(c)], 8)
        nbr, face, orient = [
            pick([t[:, class_lanes(b)] for b in range(3)], blk, lane) for t in tables
        ]
        ghost = nbr >= n_el
        inside = jnp.where(ghost, 0, nbr)
        place = pick(rank_blocks, inside >> 7, inside & 127)
        slot = jnp.where(ghost, nbr - n_el, 0)
        peer = ((slot >> 5) * 11) >> 5
        slot = peer * SLOTS + (slot & 31)
        near_ref[c] = jnp.where(ghost, SOURCES * L + slot, face * (3 * L) + place)
        sorted_orient_ref[c] = orient
        if c == 0:
            near_first_ref[...] = jnp.where(
                ghost, SOURCES * L + face * (2 * L) + slot, face * (3 * L) + place
            )
        slot = jnp.where(ghost, slot, -1)
        want = jnp.zeros((8, 2 * L), F32)
        target = lax.broadcasted_iota(I32, (2 * L, L), 0)
        for f in range(4):
            match = (jnp.broadcast_to(slot[f : f + 1], (2 * L, L)) == target).astype(F32).astype(BF16)
            value = rows_of(face[f : f + 1], 8).astype(F32).astype(BF16)
            want = want + nt_dot(value, match)
        want_ref[c : c + 1] = want[0:1]
    pad_ref[...] = jnp.zeros_like(pad_ref)
    pad_ref[:, 0:SLOTS] = jnp.maximum(send_ref[...], 0)
    quarter = lax.broadcasted_iota(I32, (1, L), 1) >> 5
    rows = []
    for g in range(3):
        for half in range(2):
            row = jnp.zeros((1, L), I32)
            for k in range(4):
                r = 3 * (4 * half + k) + g
                part = pad_ref[r : r + 1, :]
                part = pltpu.roll(part, SLOTS * k, axis=1) if k else part
                row = jnp.where(quarter == k, part, row)
            rows.append(row)
    send = jnp.concatenate(rows + rows[:2], axis=0)
    place_ref[...] = pick(rank_blocks, send >> 7, send & 127)


def run_steps(count, mats_ref, d_ref, w_ref, stack_ref, moved_ref):
    def body(k, carry):
        for q in range(Q):
            put_stack(stack_ref, q, d_ref[k, q], 64)

        def store(q, out):
            moved_ref[q, 0:KROWS] = out

        product(w_ref[0:KROWS, :], stack_ref, store)

        def put(p, r0, rn, value):
            d_ref[k + 1, p, r0 : r0 + rn, :] = value

        star_mix(mats_ref, moved_ref, put)
        return carry

    lax.fori_loop(0, count, body, 0)


def weights_between(start, end):
    return [(float(end) ** (k + 1) - float(start) ** (k + 1)) / math.factorial(k + 1) for k in range(ORDER)]


def integrate(d_ref, q, start, end):
    total = None
    for k, weight in enumerate(weights_between(start, end)):
        term = d_ref[k, q] * weight
        total = term if total is None else total + term
    return total


def traces(d_ref, w_ref, stack_ref, start, trace_ref):
    for q in range(Q):
        put_stack(stack_ref, q, integrate(d_ref, q, start, start + 1), 64)

    def store(q, out):
        trace_ref[q] = out

    product(w_ref[KROWS:WROWS, :], stack_ref, store)


def after_steps(c, d_ref, w_ref, stack_ref, own_ref, trace_refs):
    span = 2**c
    for t in range(span):
        traces(d_ref, w_ref, stack_ref, t, trace_refs[t])
    for q in range(Q):
        own_ref[q] = integrate(d_ref, q, 0, span)


def block_transpose(four, lane):
    a, b, c, d = four
    low = (lane & 64) == 0
    a, c = jnp.where(low, a, pltpu.roll(c, 64, axis=1)), jnp.where(low, pltpu.roll(a, 64, axis=1), c)
    b, d = jnp.where(low, b, pltpu.roll(d, 64, axis=1)), jnp.where(low, pltpu.roll(b, 64, axis=1), d)
    low = (lane & 32) == 0
    a, b = jnp.where(low, a, pltpu.roll(b, 32, axis=1)), jnp.where(low, pltpu.roll(a, 96, axis=1), b)
    c, d = jnp.where(low, c, pltpu.roll(d, 32, axis=1)), jnp.where(low, pltpu.roll(c, 96, axis=1), d)
    return [a, b, c, d]


def one_hot(hot_ref, index_ref, at, count, rows):
    for f in range(count):
        index = index_ref[at + f : at + f + 1, :]
        for k in range(0, rows, 2 * L):
            row = lax.broadcasted_iota(I32, (2 * L, L), 0) + k
            match = jnp.broadcast_to(index, (2 * L, L)) == row
            hot_ref[k : k + 2 * L, f * L : (f + 1) * L] = match.astype(F32).astype(BF16)


def stack_rows(ref, at, column, values, apart=HALF):
    hi, lo = split(values)
    rows = values.shape[0]
    cols = slice(column * L, (column + 1) * L)
    ref[at : at + rows, cols] = hi
    ref[apart + at : apart + at + rows, cols] = lo


def stack_quantities(lhs_ref, trace_ref, j, column):
    rows = slice(j * FP, (j + 1) * FP)
    for q in range(0, Q - 1, 2):
        two = jnp.concatenate([trace_ref[q, rows, :], trace_ref[q + 1, rows, :]], axis=0)
        stack_rows(lhs_ref, q * FP, column, two)
    stack_rows(lhs_ref, (Q - 1) * FP, column, trace_ref[Q - 1, rows, :])


def stack_traces(lhs_ref, sources):
    for b in range(3):
        for j in range(4):
            stack_quantities(lhs_ref, sources[b], j, j * 3 + b)


def both(out):
    return out[0:TROWS] + out[HALF : HALF + TROWS]


def send_tiles(dev_ref, at, tile, count, msg_ref, out_ref, cross_ref):
    place_in_group = dev_ref[0] % GROUP
    lane = lax.broadcasted_iota(I32, (8, L), 1)
    for half in range(2):
        for v in range(count):
            four = [tile(count * k + v, half) for k in range(4)]
            for k, value in enumerate(block_transpose(four, lane)):
                msg_ref[4 * half + k, v] = value
    for p in range(PEERS):
        to = place_in_group + OFFSETS[p]
        slot = (to + GROUP) % GROUP
        if abs(OFFSETS[p]) < REACH:
            out_ref[slot, at] = msg_ref[p]
            continue
        within = jnp.logical_and(to >= 0, to < GROUP)

        @pl.when(within)
        def _():
            out_ref[slot, at] = msg_ref[p]

        @pl.when(jnp.logical_not(within))
        def _():
            cross_ref[0, at] = msg_ref[p]


def receive_tiles(dev_ref, at, count, got, put):
    got_ref, cross_ref, far_ref = got
    place_in_group = dev_ref[0] % GROUP
    first = jnp.where(place_in_group < REACH, REACH + 1, 0)
    lane = lax.broadcasted_iota(I32, (8, L), 1)
    for half in range(2):
        found = []
        for k in range(4):
            offset = OFFSETS[4 * half + k]
            source = place_in_group + offset
            within = jnp.logical_and(source >= 0, source < GROUP)
            slot = (source + GROUP) % GROUP
            near = got_ref[slot, at]
            if abs(offset) == REACH:
                other = cross_ref[0, at]
            else:
                other = far_ref[jnp.clip(slot - first, 0, REACH - 2), at]
            found.append(jnp.where(within, near, other))
        for v in range(count):
            moved = block_transpose([found[k][v] for k in range(4)], lane)
            for k in range(4):
                put(count * k + v, half, moved[k])


def pack(dev_ref, rows, send_ref, hot_ref, gat_ref, msg_ref, out_ref, cross_ref):
    for at, (g, lhs_ref) in enumerate(rows):
        one_hot(hot_ref, send_ref, 2 * g, 2, SOURCES * L)
        out = jnp.dot(lhs_ref[...], hot_ref[0 : SOURCES * L, 0 : 2 * L], preferred_element_type=F32)
        gat_ref[:, 0 : 2 * L] = both(out)

        def tile(t, half):
            if t < TILES:
                return gat_ref[8 * t : 8 * t + 8, class_lanes(half)]
            return jnp.zeros((8, L), F32)

        send_tiles(dev_ref, at, tile, MSG, msg_ref, out_ref, cross_ref)


def unpack(dev_ref, at, got, gat_ref, ghost_ref):
    def put(t, half, value):
        if t < TILES:
            gat_ref[8 * t : 8 * t + 8, class_lanes(half)] = value

    receive_tiles(dev_ref, at, MSG, got, put)
    for half in range(2):
        stack_rows(ghost_ref, 0, half, gat_ref[:, class_lanes(half)])


def unpack_first(dev_ref, got, place_ref, send_ref, whole_ref, w_ref, stack_ref, trace_ref, ghost_ref):
    def put(t, half, value):
        if t < TILES0:
            whole_ref[half, t // 7, 8 * (t % 7) : 8 * (t % 7) + 8, :] = value
            return
        for g in range(3):
            row = 2 * g + half
            send_ref[row : row + 1] = value[g : g + 1].astype(I32) * (3 * L) + place_ref[row : row + 1]

    receive_tiles(dev_ref, 0, MSG0, got, put)
    send_ref[6:8] = place_ref[6:8]
    for half in range(2):
        for q in range(Q):
            put_stack(stack_ref, q, whole_ref[half, q], 64)

        def store(q, out):
            trace_ref[q] = out

        product(w_ref[KROWS:WROWS, :], stack_ref, store)
        for j in range(4):
            stack_quantities(ghost_ref, trace_ref, j, 2 * j + half)


def correct(
    state_ref, own_ref, lhs_ref, ghost_ref, index_ref, orient_ref, mats_ref, w_ref, ow_ref, lw_ref,
    stack_ref, moved_ref, hot_ref, gat_ref, cstack_ref, near_ref, flux_ref, fstack_ref, new_ref,
):
    for q in range(Q):
        put_stack(stack_ref, q, own_ref[q], 64)

    def store(q, out):
        moved_ref[q] = out

    product(w_ref[...], stack_ref, store)

    def put(p, r0, rn, value):
        new_ref[p, r0 : r0 + rn, :] = state_ref[p, r0 : r0 + rn, :] + value

    star_mix(mats_ref, moved_ref, put)
    ghosts = ghost_ref.shape[1]
    one_hot(hot_ref, index_ref, 0, 4, SOURCES * L + ghosts)
    out = jnp.dot(lhs_ref[...], hot_ref[0 : SOURCES * L, :], preferred_element_type=F32)
    out = out + jnp.dot(ghost_ref[...], hot_ref[SOURCES * L : SOURCES * L + ghosts, :], preferred_element_type=F32)
    gat_ref[...] = both(out)
    for f in range(4):
        for q in range(Q):
            put_stack(cstack_ref, q, gat_ref[q * FP : (q + 1) * FP, f * L : (f + 1) * L], 32)
        turn = rows_of(orient_ref[f : f + 1, :], FP)

        def store_near(q, out):
            value = jnp.where(turn == 1, out[FP : 2 * FP], out[0:FP])
            near_ref[q, f * FP : (f + 1) * FP] = jnp.where(turn == 2, out[2 * FP :], value)

        product(ow_ref[...], cstack_ref, store_near)

    def flux_body(f, carry):
        acc = [None] * Q
        r = pl.multiple_of(f * FP, 8)
        for q in range(Q):
            mine = moved_ref[q, pl.ds(KROWS + r, FP), :].reshape(3, 8, L)
            theirs = near_ref[q, pl.ds(r, FP), :].reshape(3, 8, L)
            for p in range(Q):
                term = row_bcast(mats_ref, p * Q + q, f) * mine
                acc[p] = term if acc[p] is None else acc[p] + term
                acc[p] = acc[p] + row_bcast(mats_ref, p * Q + q, NEIGH + f) * theirs
        for p in range(Q):
            flux_ref[p, pl.ds(r, FP), :] = acc[p].reshape(FP, L)
        return carry

    lax.fori_loop(0, 4, flux_body, 0)
    for p in range(Q):
        put_stack(fstack_ref, p, flux_ref[p], 96)

    def subtract(p, out):
        new_ref[p] = new_ref[p] - out

    product(lw_ref[...], fstack_ref, subtract, contract=0)


def first_kernel(*refs):
    dev_ref = refs[0]
    hbm = refs[1:13]
    (
        s0, s1, s2, mats, own0, own1, own2, t00, t10, t11, t20, t21, t22, t23, lhs_ref,
        near_ref, near_first_ref, sorted_orient_ref, rank_ref, place_ref, w_ref, ow_ref, lw_ref,
        out_ref, cross_ref,
    ) = refs[13:38]
    local = refs[38:50]
    (
        sems, order_ref, want_ref, wf_ref, owf_ref, lwf_ref, pad_ref,
        d_ref, stack_ref, moved_ref, hot_ref, jl_ref, gat_ref, msg_ref,
    ) = refs[50:]
    copies = [pltpu.make_async_copy(a, b, sems.at[i]) for i, (a, b) in enumerate(zip(hbm, local))]
    for copy in copies:
        copy.start()
    for copy in copies[:8]:
        copy.wait()
    make_indices(
        *local[:8], order_ref, rank_ref, near_ref, near_first_ref, sorted_orient_ref, place_ref, want_ref,
        w_ref, ow_ref, lw_ref, wf_ref, owf_ref, lwf_ref, pad_ref,
    )
    for copy in copies[8:]:
        copy.wait()
    state_ref, star_ref, fl_ref, fn_ref = local[8:]
    picks = []
    for c in range(3):
        picks.append((order_ref[0:1, class_lanes(c)], order_ref[1:2, class_lanes(c)]))
    states = [s0, s1, s2]

    def sort_rows(blocks, put):
        rows = blocks[0].shape[0]
        for c in range(3):
            put(c, pick(blocks, rows_of(picks[c][0], rows), rows_of(picks[c][1], rows)))

    def sort_state(q, carry):
        def put(c, value):
            states[c][q] = value
            d_ref[c, 0, q] = value

        sort_rows([state_ref[q, :, class_lanes(b)] for b in range(3)], put)
        return carry

    lax.fori_loop(0, Q, sort_state, 0)

    def sort_matrices(p, carry):
        for q in range(Q):
            at = p * Q + q

            def put_flux(c, value):
                mats[c, at, 0:8, :] = value

            def put_star(c, value):
                mats[c, at, STAR : STAR + 3, :] = value

            sort_rows(
                [
                    jnp.concatenate([fl_ref[p, q, :, class_lanes(b)], fn_ref[p, q, :, class_lanes(b)]], axis=0)
                    for b in range(3)
                ],
                put_flux,
            )
            sort_rows([star_ref[p, q, :, class_lanes(b)] for b in range(3)], put_star)
        return carry

    lax.fori_loop(0, Q, sort_matrices, 0)

    def each(c, carry):
        run_steps(ORDER - 1, mats.at[c], d_ref.at[c], w_ref, stack_ref, moved_ref)
        return carry

    lax.fori_loop(0, 3, each, 0)
    after_steps(0, d_ref.at[0], w_ref, stack_ref, own0, [t00])
    after_steps(1, d_ref.at[1], w_ref, stack_ref, own1, [t10, t11])
    after_steps(2, d_ref.at[2], w_ref, stack_ref, own2, [t20, t21, t22, t23])
    stack_traces(lhs_ref, [t00, t10, t20])
    for c in range(3):
        for q in range(0, Q, 2):
            parts = [integrate(d_ref.at[c], r, 0, 1) for r in range(q, min(q + 2, Q))]
            stack_rows(jl_ref, q * B, c, jnp.concatenate(parts, axis=0), HALF0)
    one_hot(hot_ref, place_ref, 0, 2, 3 * L)
    out = jnp.dot(jl_ref[...], hot_ref[0 : 3 * L, 0 : 2 * L], preferred_element_type=F32)
    gat_ref[...] = out[0 : Q * B] + out[HALF0 : HALF0 + Q * B]

    def tile(t, half):
        if t < TILES0:
            return gat_ref[8 * t : 8 * t + 8, class_lanes(half)]
        return want_ref[:, class_lanes(half)]

    send_tiles(dev_ref, 0, tile, MSG0, msg_ref, out_ref, cross_ref)


def step_kernel(n, *refs):
    refs = list(refs)

    def take(count):
        got = refs[:count]
        del refs[:count]
        return got

    ending = [c for c in range(3) if n % 2**c == 0]
    sending = [c for c in range(3) if (n + 1) % 2**c == 0] if n < STEPS else []
    last = n == STEPS
    (dev_ref,) = take(1)
    got = take(3)
    index_ref, orient_ref = take(2)
    (mats,) = take(1)
    w_ref, ow_ref, lw_ref = take(3)
    states = dict((c, take(1)[0]) for c in ending)
    owns = dict((c, take(1)[0]) for c in ending)
    sources = dict((c, take(1)[0]) for c in ending)
    if last:
        (rank_ref,) = take(1)
        final_ref, energy_ref = take(2)
        news = None
    else:
        kept = dict((c, take(1)[0]) for c in range(3) if c not in ending)
        before = take(3) if n % 2 == 1 else None
        half_sums = take(3) if n == 3 else None
        near_first_ref, place_ref = take(2) if n == 1 else (None, None)
        send_ref = take(1)[0] if n > 1 else None
        news = dict((c, take(1)[0]) for c in ending)
        new_owns = dict((c, take(1)[0]) for c in ending)
        new_traces = dict((c, take(2**c)) for c in ending)
        sums = take(3) if n == 1 else None
        lhs = dict((c, take(1)[0]) for c in sending)
        if n == 1:
            (send_ref,) = take(1)
        out_ref, cross_ref = take(2)
    ghost_ref, stack_ref, moved_ref, hot_ref, gat_ref, cstack_ref, near_ref, flux_ref, fstack_ref = take(9)
    if last:
        (new_scratch,) = take(1)
        news = dict((c, new_scratch.at[c]) for c in range(3))
    else:
        d_ref, msg_ref = take(2)
        if n == 3:
            sums = take(3)
        if n == 1:
            (whole_ref,) = take(1)
    for at, c in enumerate(ending):
        if n == 1:
            unpack_first(
                dev_ref, got, place_ref, send_ref, whole_ref, w_ref, stack_ref, near_ref, ghost_ref
            )
        else:
            unpack(dev_ref, at, got, gat_ref.at[:, 0 : 2 * L], ghost_ref)
        correct(
            states[c], owns[c], sources[c], ghost_ref, near_first_ref if n == 1 else index_ref.at[c], orient_ref.at[c],
            mats.at[c], w_ref, ow_ref, lw_ref,
            stack_ref, moved_ref, hot_ref, gat_ref, cstack_ref, near_ref, flux_ref, fstack_ref, news[c],
        )
    if last:
        total = jnp.zeros((8, L), F32)
        for c in range(3):
            for q in range(Q):
                v = news[c][q]
                total = total + jnp.sum((v * v).reshape(B // 8, 8, L), axis=0)
        line = jnp.sum(total, axis=0, keepdims=True)
        energy_ref[...] = jnp.broadcast_to(line[None], energy_ref.shape)
        for b in range(3):
            blk = rows_of(rank_ref[0:1, class_lanes(b)], B)
            index = rows_of(rank_ref[1:2, class_lanes(b)], B)

            def unsort(q, carry):
                final_ref[q, :, class_lanes(b)] = pick([news[c][q] for c in range(3)], blk, index)
                return carry

            lax.fori_loop(0, Q, unsort, 0)
        return
    for c in ending:
        for q in range(Q):
            d_ref[0, q] = news[c][q]
        run_steps(ORDER - 1, mats.at[c], d_ref, w_ref, stack_ref, moved_ref)
        after_steps(c, d_ref, w_ref, stack_ref, new_owns[c], new_traces[c])
    now = [new_traces[c][0] if c in ending else kept[c] for c in range(3)]
    stack_traces(lhs[0], now)
    if sums is not None:
        for b in range(3):
            for q in range(Q):
                sums[b][q] = before[b][q] + now[b][q]
        stack_traces(lhs[1], sums)
    if n == 3:
        for b in range(3):
            for q in range(Q):
                sums[b][q] = sums[b][q] + half_sums[b][q]
        stack_traces(lhs[2], sums)
    pack(dev_ref, [(g, lhs[g]) for g in sending], send_ref, hot_ref, gat_ref, msg_ref, out_ref, cross_ref)


FIELD = (Q, B, L)
TRACE = (Q, 4 * FP, L)


def shards(
    state, class_label, stiffness, star, face_proj, orient_map, flux_local, flux_neigh,
    neighbor, neighbor_face, orientation, send_list,
):
    elements = state.shape[2]
    devices = lax.axis_size("dom")
    aligned = [[GROUP * k + i for i in range(GROUP)] for k in range(devices // GROUP)]
    across = [(d, (d - REACH if d % GROUP < REACH else d + REACH) % devices) for d in range(devices)]
    onward = [(d, (d + GROUP if d % GROUP < REACH else d - GROUP) % devices) for d in range(devices)]
    axis_index = lax.axis_index("dom").astype(I32)
    exit_first = jnp.where(axis_index % GROUP < REACH, REACH + 1, 0).astype(I32)
    axis_index, exit_first = lax.optimization_barrier((axis_index, exit_first))

    def exchange(out, cross):
        got_cross = lax.ppermute(cross, "dom", across)
        got = lax.all_to_all(out, "dom", 0, 0, axis_index_groups=aligned, tiled=True)
        far = lax.dynamic_slice_in_dim(got, exit_first, REACH - 1, 0, allow_negative_indices=False)
        return got, got_cross, lax.ppermute(far, "dom", onward)

    dev = axis_index.reshape(1)
    smem = pl.BlockSpec(memory_space=pltpu.SMEM)
    whole = pl.BlockSpec(memory_space=pltpu.VMEM)
    stay = pl.BlockSpec(memory_space=pltpu.HBM)

    def run(kernel, args, outs, scratch, name, rest=whole):
        return pl.pallas_call(
            kernel,
            in_specs=[smem] + [rest] * (len(args) - 1),
            out_specs=[whole] * len(outs),
            out_shape=outs,
            scratch_shapes=scratch,
            compiler_params=pltpu.CompilerParams(vmem_limit_bytes=VMEM_LIMIT),
            name=name,
        )(*args)

    stack = pltpu.VMEM((192, Q * L), BF16)
    moved = pltpu.VMEM((Q, WROWS, L), F32)
    gat = pltpu.VMEM((TROWS, 4 * L), F32)
    stacked = shape((2 * HALF, SOURCES * L), BF16)

    def hot(ghosts):
        return pltpu.VMEM(((SOURCES + ghosts) * L, 4 * L), BF16)

    def msg(count):
        return pltpu.VMEM((PEERS, count, 8, L), F32)

    def messages(rows, count):
        return [shape((GROUP, rows, count, 8, L)), shape((1, rows, count, 8, L))]

    def matrices(array):
        return array.transpose(1, 2, 0, 3)

    inputs = [
        class_label.reshape(3, L), neighbor, neighbor_face, orientation, send_list, stiffness,
        face_proj.transpose(1, 0, 2), orient_map,
        state, matrices(star), matrices(flux_local), matrices(flux_neigh),
    ]
    got = list(
        run(
            first_kernel,
            [dev] + inputs,
            [shape(FIELD)] * 3 + [shape((3, Q * Q, 16, L))] + [shape(FIELD)] * 3 + [shape(TRACE)] * 7 + [stacked]
            + [shape((3, 8, L), I32), shape((8, L), I32), shape((3, 8, L), I32), shape((8, elements), I32), shape((8, L), I32)]
            + [shape((WROWS, 192), BF16), shape((3 * FP, 96), BF16), shape((288, B), BF16)]
            + messages(1, MSG0),
            [pltpu.VMEM(x.shape, x.dtype) for x in inputs]
            + [
                pltpu.SemaphoreType.DMA((len(inputs),)),
                pltpu.VMEM((8, elements), I32), pltpu.VMEM((8, 2 * L), F32),
                pltpu.VMEM((WROWS, 192), F32), pltpu.VMEM((3 * FP, 96), F32), pltpu.VMEM((288, B), F32),
                pltpu.VMEM((3 * PEERS, L), I32),
                pltpu.VMEM((3, ORDER) + FIELD, F32), stack, moved, pltpu.VMEM((4 * L, 2 * L), BF16),
                pltpu.VMEM((2 * HALF0, 3 * L), BF16), pltpu.VMEM((Q * B, 2 * L), F32), msg(MSG0),
            ],
            "first",
            rest=stay,
        )
    )
    fields = got[0:3]
    mats = got[3]
    owns = got[4:7]
    t00, t10, t11, t20, t21, t22, t23, lhs = got[7:15]
    near, near_first, orient, rank, place, w, ow, lw, out, cross = got[15:]
    later = {1: {0: t10, 1: t11}, 2: {0: t20, 1: t21, 2: t22, 3: t23}}
    now = [t00, t10, t20]
    sources = {0: lhs}
    half_sums = None
    for n in range(1, STEPS + 1):
        ending = [c for c in range(3) if n % 2**c == 0]
        args = [dev, *exchange(out, cross), near, orient, mats, w, ow, lw]
        args += [fields[c] for c in ending] + [owns[c] for c in ending] + [sources[c] for c in ending]
        common = [
            pltpu.VMEM((2 * HALF, (8 if n == 1 else 2) * L), BF16), stack, moved, hot(8 if n == 1 else 2), gat, pltpu.VMEM((96, Q * L), BF16),
            pltpu.VMEM(TRACE, F32), pltpu.VMEM(TRACE, F32), pltpu.VMEM((288, Q * L), BF16),
        ]

        def kernel(*refs, n=n):
            step_kernel(n, *refs)

        if n == STEPS:
            final_state, energy_out = run(
                kernel,
                args + [rank],
                [shape((Q, B, elements)), shape((devices, 1, L))],
                common + [pltpu.VMEM((3,) + FIELD, F32)],
                "last",
            )
            break
        sending = [c for c in range(3) if (n + 1) % 2**c == 0]
        kept = [c for c in range(3) if c not in ending]
        args += [later[c][n % 2**c] for c in kept]
        if n % 2 == 1:
            args += now
        if n == 3:
            args += half_sums
        args += [near_first, place] if n == 1 else [send_index]
        outs = [shape(FIELD)] * (2 * len(ending)) + [shape(TRACE)] * sum(2**c for c in ending)
        outs += [shape(TRACE)] * (3 if n == 1 else 0) + [stacked] * len(sending)
        outs += [shape((8, L), I32)] if n == 1 else []
        outs += messages(len(sending), MSG)
        scratch = common + [pltpu.VMEM((ORDER,) + FIELD, F32), msg(MSG)]
        scratch += [pltpu.VMEM(TRACE, F32)] * (3 if n == 3 else 0)
        scratch += [pltpu.VMEM((2,) + FIELD, F32)] if n == 1 else []
        got = list(run(kernel, args, outs, scratch, "step%d" % n))
        for c in ending:
            fields[c] = got.pop(0)
        for c in ending:
            owns[c] = got.pop(0)
        for c in ending:
            made = [got.pop(0) for _ in range(2**c)]
            later[c] = dict(enumerate(made))
        now = [later[c][n % 2**c] for c in range(3)]
        if n == 1:
            half_sums = [got.pop(0) for _ in range(3)]
        for c in sending:
            sources[c] = got.pop(0)
        if n == 1:
            send_index = got.pop(0)
        out, cross = got
    spread = lax.all_to_all(energy_out, "dom", 0, 0, tiled=True)
    energy = jnp.sum(spread).reshape(1) / (devices * elements * Q * B)
    return final_state, energy


def solution(mesh):
    in_specs = (
        P(None, None, "dom"),
        P("dom"),
        P(),
        P(None, None, None, "dom"),
        P(),
        P(),
        P(None, None, None, "dom"),
        P(None, None, None, "dom"),
        P(None, "dom"),
        P(None, "dom"),
        P(None, "dom"),
        P("dom", None),
    )
    out_specs = (P(None, None, "dom"), P())
    return jax.shard_map(shards, mesh=mesh, in_specs=in_specs, out_specs=out_specs, check_vma=False)
```

```python
import math

import jax
import jax.numpy as jnp
from jax import lax
from jax.experimental import pallas as pl
from jax.experimental.pallas import tpu as pltpu
from jax.sharding import PartitionSpec as P

ORDER = 6
Q = 9
B = 56
FB = 21
FP = 24
L = 128
REACH = 4
PEERS = 8
SLOTS = 32
GROUP = 8
STEPS = 4
OFFSETS = [p - REACH if p < REACH else p - REACH + 1 for p in range(PEERS)]
KROWS = 3 * B
WROWS = KROWS + 4 * FP
MSG = 7
HALF = 224
MSG0 = 16
HALF0 = 512
TILES = 3 * Q
TILES0 = 7 * Q
TROWS = Q * FP
SOURCES = 12
NEIGH = 4
STAR = 8
F32 = jnp.float32
BF16 = jnp.bfloat16
I32 = jnp.int32
VMEM_LIMIT = 40 * 1024 * 1024


def shape(dims, dtype=F32):
    return jax.ShapeDtypeStruct(dims, dtype)


def lane_take(x, index):
    numbers = lax.GatherDimensionNumbers(
        offset_dims=(),
        collapsed_slice_dims=(1,),
        start_index_map=(1,),
        operand_batching_dims=(0,),
        start_indices_batching_dims=(0,),
    )
    return lax.gather(
        x,
        index[..., None],
        numbers,
        slice_sizes=(1, 1),
        mode=lax.GatherScatterMode.PROMISE_IN_BOUNDS,
    )


def pick(blocks, code, lane):
    out = lane_take(blocks[0], lane)
    for k in range(1, len(blocks)):
        out = jnp.where(code == k, lane_take(blocks[k], lane), out)
    return out


def rows_of(vec, rows):
    return jnp.broadcast_to(vec, (rows, L))


def split(values):
    hi = values.astype(BF16)
    lo = (values - hi.astype(F32)).astype(BF16)
    return hi, lo


def put_stack(ref, q, values, rows):
    have = values.shape[0]
    if have < rows:
        values = jnp.concatenate([values, jnp.zeros((rows - have, L), F32)], axis=0)
    hi, lo = split(values)
    cols = slice(q * L, (q + 1) * L)
    ref[0:rows, cols] = hi
    ref[rows : 2 * rows, cols] = lo
    ref[2 * rows : 3 * rows, cols] = hi


def column_tiles():
    return [(t, min(2, Q - t)) for t in range(0, Q, 2)]


def product(weights, stack_ref, store, contract=1):
    for start, count in column_tiles():
        cols = slice(start * L, (start + count) * L)
        out = lax.dot_general(
            weights,
            stack_ref[:, cols],
            (((contract,), (0,)), ((), ())),
            preferred_element_type=F32,
        )
        for j in range(count):
            store(start + j, out[:, j * L : (j + 1) * L])


def mix_groups(total, most):
    groups = []
    at = 0
    while at < total:
        size = min(most, total - at)
        groups.append((at, size))
        at += size
    return groups


def row_bcast(ref, at, row):
    return jnp.broadcast_to(ref[at, pl.ds(row, 1), :], (8, L))[None]


def star_mix(mats_ref, moved_ref, put):
    for r0, rn in mix_groups(B, 32):
        acc = [None] * Q
        for d in range(3):
            for q in range(Q):
                m = moved_ref[q, d * B + r0 : d * B + r0 + rn, :].reshape(rn // 8, 8, L)
                for p in range(Q):
                    term = row_bcast(mats_ref, p * Q + q, STAR + d) * m
                    acc[p] = term if acc[p] is None else acc[p] + term
        for p in range(Q):
            put(p, r0, rn, acc[p].reshape(rn, L))


def class_lanes(c):
    return slice(c * L, (c + 1) * L)


def nt_dot(a, b):
    return lax.dot_general(a, b, (((1,), (1,)), ((), ())), preferred_element_type=F32)


def make_indices(
    label_ref, nbr_ref, face_ref, orient_ref, send_ref, stiff_ref, proj_ref, omap_ref,
    order_ref, rank_ref, near_ref, near_first_ref, sorted_orient_ref, place_ref, want_ref,
    w_ref, ow_ref, lw_ref, wf_ref, owf_ref, lwf_ref, pad_ref,
):
    n_el = nbr_ref.shape[1]
    wf_ref[...] = jnp.zeros_like(wf_ref)
    owf_ref[...] = jnp.zeros_like(owf_ref)
    for d in range(3):
        k = stiff_ref[d]
        hi = k.astype(BF16).astype(F32)
        rows = slice(d * B, (d + 1) * B)
        wf_ref[rows, 0:B] = hi
        wf_ref[rows, 64 : 64 + B] = hi
        wf_ref[rows, 128 : 128 + B] = k - hi
    lwf_ref[...] = jnp.zeros_like(lwf_ref)
    for j in range(4):
        k = proj_ref[:, j, :]
        hi = k.astype(BF16).astype(F32)
        rows = slice(KROWS + j * FP, KROWS + j * FP + FB)
        wf_ref[rows, 0:B] = hi
        wf_ref[rows, 64 : 64 + B] = hi
        wf_ref[rows, 128 : 128 + B] = k - hi
        lwf_ref[j * FP : j * FP + FB, :] = hi
        lwf_ref[96 + j * FP : 96 + j * FP + FB, :] = hi
        lwf_ref[192 + j * FP : 192 + j * FP + FB, :] = k - hi
    for h in range(3):
        k = omap_ref[h]
        hi = k.astype(BF16).astype(F32)
        rows = slice(h * FP, h * FP + FB)
        owf_ref[rows, 0:FB] = hi
        owf_ref[rows, 32 : 32 + FB] = hi
        owf_ref[rows, 64 : 64 + FB] = k - hi
    w_ref[...] = wf_ref[...].astype(BF16)
    ow_ref[...] = owf_ref[...].astype(BF16)
    lw_ref[...] = lwf_ref[...].astype(BF16)
    label = jnp.concatenate([label_ref[c : c + 1, :] for c in range(3)], axis=1)
    classes = lax.broadcasted_iota(I32, (8, n_el), 0)
    hot = (jnp.broadcast_to(label, (8, n_el)) == classes).astype(F32)
    row = lax.broadcasted_iota(I32, (n_el, n_el), 0)
    col = lax.broadcasted_iota(I32, (n_el, n_el), 1)
    before = (row < col).astype(F32).astype(BF16)
    prefix = jnp.dot(hot.astype(BF16), before, preferred_element_type=F32)
    base = classes.astype(F32) * float(L)
    rank = jnp.sum(hot * (prefix + base), axis=0, keepdims=True).astype(I32)
    here = (jnp.broadcast_to(rank, (n_el, n_el)) == row).astype(F32).astype(BF16)
    ids = lax.broadcasted_iota(I32, (8, n_el), 1)
    first = lax.broadcasted_iota(I32, (8, n_el), 0) == 0
    parts = jnp.where(first, ids // L, ids % L).astype(F32).astype(BF16)
    order = nt_dot(parts, here).astype(I32)
    order_ref[...] = order
    rank_ref[...] = jnp.where(first, jnp.broadcast_to(rank >> 7, (8, n_el)), jnp.broadcast_to(rank & 127, (8, n_el)))
    rank_blocks = [rows_of(rank[:, class_lanes(c)], 8) for c in range(3)]
    pad = jnp.zeros((4, n_el), I32)
    tables = [jnp.concatenate([ref[...], pad], axis=0) for ref in (nbr_ref, face_ref, orient_ref)]
    want_ref[...] = jnp.zeros_like(want_ref)
    for c in range(3):
        blk = rows_of(order[0:1, class_lanes(c)], 8)
        lane = rows_of(order[1:2, class_lanes(c)], 8)
        nbr, face, orient = [
            pick([t[:, class_lanes(b)] for b in range(3)], blk, lane) for t in tables
        ]
        ghost = nbr >= n_el
        inside = jnp.where(ghost, 0, nbr)
        place = pick(rank_blocks, inside >> 7, inside & 127)
        slot = jnp.where(ghost, nbr - n_el, 0)
        peer = ((slot >> 5) * 11) >> 5
        slot = peer * SLOTS + (slot & 31)
        near_ref[c] = jnp.where(ghost, SOURCES * L + slot, face * (3 * L) + place)
        sorted_orient_ref[c] = orient
        if c == 0:
            near_first_ref[...] = jnp.where(
                ghost, SOURCES * L + face * (2 * L) + slot, face * (3 * L) + place
            )
        slot = jnp.where(ghost, slot, -1)
        want = jnp.zeros((8, 2 * L), F32)
        target = lax.broadcasted_iota(I32, (2 * L, L), 0)
        for f in range(4):
            match = (jnp.broadcast_to(slot[f : f + 1], (2 * L, L)) == target).astype(F32).astype(BF16)
            value = rows_of(face[f : f + 1], 8).astype(F32).astype(BF16)
            want = want + nt_dot(value, match)
        want_ref[c : c + 1] = want[0:1]
    pad_ref[...] = jnp.zeros_like(pad_ref)
    pad_ref[:, 0:SLOTS] = jnp.maximum(send_ref[...], 0)
    quarter = lax.broadcasted_iota(I32, (1, L), 1) >> 5
    rows = []
    for g in range(3):
        for half in range(2):
            row = jnp.zeros((1, L), I32)
            for k in range(4):
                r = 3 * (4 * half + k) + g
                part = pad_ref[r : r + 1, :]
                part = pltpu.roll(part, SLOTS * k, axis=1) if k else part
                row = jnp.where(quarter == k, part, row)
            rows.append(row)
    send = jnp.concatenate(rows + rows[:2], axis=0)
    place_ref[...] = pick(rank_blocks, send >> 7, send & 127)


def run_steps(count, mats_ref, d_ref, w_ref, stack_ref, moved_ref):
    def body(k, carry):
        for q in range(Q):
            put_stack(stack_ref, q, d_ref[k, q], 64)

        def store(q, out):
            moved_ref[q, 0:KROWS] = out

        product(w_ref[0:KROWS, :], stack_ref, store)

        def put(p, r0, rn, value):
            d_ref[k + 1, p, r0 : r0 + rn, :] = value

        star_mix(mats_ref, moved_ref, put)
        return carry

    lax.fori_loop(0, count, body, 0)


def weights_between(start, end):
    return [(float(end) ** (k + 1) - float(start) ** (k + 1)) / math.factorial(k + 1) for k in range(ORDER)]


def integrate(d_ref, q, start, end):
    total = None
    for k, weight in enumerate(weights_between(start, end)):
        term = d_ref[k, q] * weight
        total = term if total is None else total + term
    return total


def traces(d_ref, w_ref, stack_ref, start, trace_ref):
    for q in range(Q):
        put_stack(stack_ref, q, integrate(d_ref, q, start, start + 1), 64)

    def store(q, out):
        trace_ref[q] = out

    product(w_ref[KROWS:WROWS, :], stack_ref, store)


def after_steps(c, d_ref, w_ref, stack_ref, own_ref, trace_refs):
    span = 2**c
    for t in range(span):
        traces(d_ref, w_ref, stack_ref, t, trace_refs[t])
    for q in range(Q):
        own_ref[q] = integrate(d_ref, q, 0, span)


def block_transpose(four, lane):
    a, b, c, d = four
    low = (lane & 64) == 0
    a, c = jnp.where(low, a, pltpu.roll(c, 64, axis=1)), jnp.where(low, pltpu.roll(a, 64, axis=1), c)
    b, d = jnp.where(low, b, pltpu.roll(d, 64, axis=1)), jnp.where(low, pltpu.roll(b, 64, axis=1), d)
    low = (lane & 32) == 0
    a, b = jnp.where(low, a, pltpu.roll(b, 32, axis=1)), jnp.where(low, pltpu.roll(a, 96, axis=1), b)
    c, d = jnp.where(low, c, pltpu.roll(d, 32, axis=1)), jnp.where(low, pltpu.roll(c, 96, axis=1), d)
    return [a, b, c, d]


def one_hot(hot_ref, index_ref, at, count, rows, first=0):
    for f in range(count):
        index = index_ref[at + f : at + f + 1, :]
        for k in range(0, rows, 2 * L):
            row = lax.broadcasted_iota(I32, (2 * L, L), 0) + (first + k)
            match = jnp.broadcast_to(index, (2 * L, L)) == row
            hot_ref[k : k + 2 * L, f * L : (f + 1) * L] = match.astype(F32).astype(BF16)


def stack_rows(ref, at, column, values, apart=HALF):
    hi, lo = split(values)
    rows = values.shape[0]
    cols = slice(column * L, (column + 1) * L)
    ref[at : at + rows, cols] = hi
    ref[apart + at : apart + at + rows, cols] = lo


def stack_quantities(lhs_ref, trace_ref, j, column):
    rows = slice(j * FP, (j + 1) * FP)
    for q in range(0, Q - 1, 2):
        two = jnp.concatenate([trace_ref[q, rows, :], trace_ref[q + 1, rows, :]], axis=0)
        stack_rows(lhs_ref, q * FP, column, two)
    stack_rows(lhs_ref, (Q - 1) * FP, column, trace_ref[Q - 1, rows, :])


def stack_traces(lhs_ref, sources):
    for b in range(3):
        for j in range(4):
            stack_quantities(lhs_ref, sources[b], j, j * 3 + b)


def both(out):
    return out[0:TROWS] + out[HALF : HALF + TROWS]


def send_tiles(dev_ref, at, tile, count, msg_ref, out_ref, cross_ref):
    place_in_group = dev_ref[0] % GROUP
    lane = lax.broadcasted_iota(I32, (8, L), 1)
    for half in range(2):
        for v in range(count):
            four = [tile(count * k + v, half) for k in range(4)]
            for k, value in enumerate(block_transpose(four, lane)):
                msg_ref[4 * half + k, v] = value
    for p in range(PEERS):
        to = place_in_group + OFFSETS[p]
        slot = (to + GROUP) % GROUP
        if abs(OFFSETS[p]) < REACH:
            out_ref[slot, at] = msg_ref[p]
            continue
        within = jnp.logical_and(to >= 0, to < GROUP)

        @pl.when(within)
        def _():
            cross_ref[0, at] = msg_ref[p]

        @pl.when(jnp.logical_not(within))
        def _():
            out_ref[slot, at] = msg_ref[p]


def receive_tiles(dev_ref, at, count, got, put):
    got_ref, cross_ref, far_ref = got
    place_in_group = dev_ref[0] % GROUP
    first = jnp.where(place_in_group < REACH, REACH, 0)
    lane = lax.broadcasted_iota(I32, (8, L), 1)
    for half in range(2):
        found = []
        for k in range(4):
            offset = OFFSETS[4 * half + k]
            source = place_in_group + offset
            within = jnp.logical_and(source >= 0, source < GROUP)
            slot = (source + GROUP) % GROUP
            near = cross_ref[0, at] if abs(offset) == REACH else got_ref[slot, at]
            other = far_ref[jnp.clip(slot - first, 0, REACH - 1), at]
            found.append(jnp.where(within, near, other))
        for v in range(count):
            moved = block_transpose([found[k][v] for k in range(4)], lane)
            for k in range(4):
                put(count * k + v, half, moved[k])


def pack(dev_ref, rows, send_ref, hot_ref, gat_ref, msg_ref, out_ref, cross_ref):
    for at, (g, lhs_ref) in enumerate(rows):
        one_hot(hot_ref, send_ref, 2 * g, 2, SOURCES * L)
        out = jnp.dot(lhs_ref[...], hot_ref[0 : SOURCES * L, 0 : 2 * L], preferred_element_type=F32)
        gat_ref[:, 0 : 2 * L] = both(out)

        def tile(t, half):
            if t < TILES:
                return gat_ref[8 * t : 8 * t + 8, class_lanes(half)]
            return jnp.zeros((8, L), F32)

        send_tiles(dev_ref, at, tile, MSG, msg_ref, out_ref, cross_ref)


def unpack(dev_ref, at, got, gat_ref, ghost_ref):
    def put(t, half, value):
        if t < TILES:
            gat_ref[8 * t : 8 * t + 8, class_lanes(half)] = value

    receive_tiles(dev_ref, at, MSG, got, put)
    for half in range(2):
        stack_rows(ghost_ref, 0, half, gat_ref[:, class_lanes(half)])


def unpack_first(dev_ref, got, place_ref, send_ref, whole_ref, w_ref, stack_ref, trace_ref, ghost_ref):
    def put(t, half, value):
        if t < TILES0:
            whole_ref[half, t // 7, 8 * (t % 7) : 8 * (t % 7) + 8, :] = value
            return
        for g in range(3):
            row = 2 * g + half
            send_ref[row : row + 1] = value[g : g + 1].astype(I32) * (3 * L) + place_ref[row : row + 1]

    receive_tiles(dev_ref, 0, MSG0, got, put)
    send_ref[6:8] = place_ref[6:8]
    for half in range(2):
        for q in range(Q):
            put_stack(stack_ref, q, whole_ref[half, q], 64)

        def store(q, out):
            trace_ref[q] = out

        product(w_ref[KROWS:WROWS, :], stack_ref, store)
        for j in range(4):
            stack_quantities(ghost_ref, trace_ref, j, 2 * j + half)


def flux_mix(mats_ref, row, trace_ref, at, flux_ref, more):
    def body(f, carry):
        r = pl.multiple_of(f * FP, 8)
        acc = [flux_ref[p, pl.ds(r, FP), :].reshape(3, 8, L) if more else None for p in range(Q)]
        for q in range(Q):
            trace = trace_ref[q, pl.ds(at + r, FP), :].reshape(3, 8, L)
            for p in range(Q):
                term = row_bcast(mats_ref, p * Q + q, row + f) * trace
                acc[p] = term if acc[p] is None else acc[p] + term
        for p in range(Q):
            flux_ref[p, pl.ds(r, FP), :] = acc[p].reshape(FP, L)
        return carry

    lax.fori_loop(0, 4, body, 0)


def local_part(
    state_ref, own_ref, lhs_ref, index_ref, mats_ref, w_ref, stack_ref, moved_ref, hot_ref,
    partial_ref, flux_ref, chosen_ref,
):
    for q in range(Q):
        put_stack(stack_ref, q, own_ref[q], 64)

    def store(q, out):
        moved_ref[q] = out

    product(w_ref[...], stack_ref, store)

    def put(p, r0, rn, value):
        partial_ref[p, r0 : r0 + rn, :] = state_ref[p, r0 : r0 + rn, :] + value

    star_mix(mats_ref, moved_ref, put)
    one_hot(hot_ref, index_ref, 0, 4, SOURCES * L)
    chosen_ref[...] = both(jnp.dot(lhs_ref[...], hot_ref[...], preferred_element_type=F32))
    flux_mix(mats_ref, 0, moved_ref, KROWS, flux_ref, False)


def ghost_part(
    partial_ref, flux_ref, chosen_ref, ghost_ref, index_ref, orient_ref, mats_ref, ow_ref, lw_ref,
    hot_ref, gat_ref, cstack_ref, near_ref, sum_ref, fstack_ref, new_ref,
):
    ghosts = ghost_ref.shape[1]
    one_hot(hot_ref, index_ref, 0, 4, ghosts, SOURCES * L)
    out = jnp.dot(ghost_ref[...], hot_ref[0:ghosts, :], preferred_element_type=F32)
    gat_ref[...] = chosen_ref[...] + both(out)
    for f in range(4):
        for q in range(Q):
            put_stack(cstack_ref, q, gat_ref[q * FP : (q + 1) * FP, f * L : (f + 1) * L], 32)
        turn = rows_of(orient_ref[f : f + 1, :], FP)

        def store_near(q, out):
            value = jnp.where(turn == 1, out[FP : 2 * FP], out[0:FP])
            near_ref[q, f * FP : (f + 1) * FP] = jnp.where(turn == 2, out[2 * FP :], value)

        product(ow_ref[...], cstack_ref, store_near)
    sum_ref[...] = flux_ref[...]
    flux_mix(mats_ref, NEIGH, near_ref, 0, sum_ref, True)
    for p in range(Q):
        put_stack(fstack_ref, p, sum_ref[p], 96)

    def subtract(p, out):
        new_ref[p] = partial_ref[p] - out

    product(lw_ref[...], fstack_ref, subtract, contract=0)


def first_kernel(*refs):
    dev_ref = refs[0]
    hbm = refs[1:13]
    (
        s0, s1, s2, mats, own0, own1, own2, t00, t10, t11, t20, t21, t22, t23, lhs_ref,
        near_ref, near_first_ref, sorted_orient_ref, rank_ref, place_ref, w_ref, ow_ref, lw_ref,
        out_ref, cross_ref,
    ) = refs[13:38]
    local = refs[38:50]
    (
        sems, order_ref, want_ref, wf_ref, owf_ref, lwf_ref, pad_ref,
        d_ref, stack_ref, moved_ref, hot_ref, jl_ref, gat_ref, msg_ref,
    ) = refs[50:]
    copies = [pltpu.make_async_copy(a, b, sems.at[i]) for i, (a, b) in enumerate(zip(hbm, local))]
    for copy in copies:
        copy.start()
    for copy in copies[:8]:
        copy.wait()
    make_indices(
        *local[:8], order_ref, rank_ref, near_ref, near_first_ref, sorted_orient_ref, place_ref, want_ref,
        w_ref, ow_ref, lw_ref, wf_ref, owf_ref, lwf_ref, pad_ref,
    )
    for copy in copies[8:]:
        copy.wait()
    state_ref, star_ref, fl_ref, fn_ref = local[8:]
    picks = []
    for c in range(3):
        picks.append((order_ref[0:1, class_lanes(c)], order_ref[1:2, class_lanes(c)]))
    states = [s0, s1, s2]

    def sort_rows(blocks, put):
        rows = blocks[0].shape[0]
        for c in range(3):
            put(c, pick(blocks, rows_of(picks[c][0], rows), rows_of(picks[c][1], rows)))

    def sort_state(q, carry):
        def put(c, value):
            states[c][q] = value
            d_ref[c, 0, q] = value

        sort_rows([state_ref[q, :, class_lanes(b)] for b in range(3)], put)
        return carry

    lax.fori_loop(0, Q, sort_state, 0)

    def sort_matrices(p, carry):
        for q in range(Q):
            at = p * Q + q

            def put_flux(c, value):
                mats[c, at, 0:8, :] = value

            def put_star(c, value):
                mats[c, at, STAR : STAR + 3, :] = value

            sort_rows(
                [
                    jnp.concatenate([fl_ref[p, q, :, class_lanes(b)], fn_ref[p, q, :, class_lanes(b)]], axis=0)
                    for b in range(3)
                ],
                put_flux,
            )
            sort_rows([star_ref[p, q, :, class_lanes(b)] for b in range(3)], put_star)
        return carry

    lax.fori_loop(0, Q, sort_matrices, 0)

    def each(c, carry):
        run_steps(ORDER - 1, mats.at[c], d_ref.at[c], w_ref, stack_ref, moved_ref)
        return carry

    lax.fori_loop(0, 3, each, 0)
    after_steps(0, d_ref.at[0], w_ref, stack_ref, own0, [t00])
    after_steps(1, d_ref.at[1], w_ref, stack_ref, own1, [t10, t11])
    after_steps(2, d_ref.at[2], w_ref, stack_ref, own2, [t20, t21, t22, t23])
    stack_traces(lhs_ref, [t00, t10, t20])
    for c in range(3):
        for q in range(0, Q, 2):
            parts = [integrate(d_ref.at[c], r, 0, 1) for r in range(q, min(q + 2, Q))]
            stack_rows(jl_ref, q * B, c, jnp.concatenate(parts, axis=0), HALF0)
    one_hot(hot_ref, place_ref, 0, 2, 3 * L)
    out = jnp.dot(jl_ref[...], hot_ref[0 : 3 * L, 0 : 2 * L], preferred_element_type=F32)
    gat_ref[...] = out[0 : Q * B] + out[HALF0 : HALF0 + Q * B]

    def tile(t, half):
        if t < TILES0:
            return gat_ref[8 * t : 8 * t + 8, class_lanes(half)]
        return want_ref[:, class_lanes(half)]

    send_tiles(dev_ref, 0, tile, MSG0, msg_ref, out_ref, cross_ref)


def local_kernel(n, *refs):
    refs = list(refs)

    def take(count):
        got = refs[:count]
        del refs[:count]
        return got

    ending = [c for c in range(3) if n % 2**c == 0]
    take(2)
    index_ref, mats, w_ref = take(3)
    states, owns, sources = take(len(ending)), take(len(ending)), take(len(ending))
    partials, fluxes, chosen = take(len(ending)), take(len(ending)), take(len(ending))
    stack_ref, moved_ref, hot_ref = take(3)
    for at, c in enumerate(ending):
        local_part(
            states[at], owns[at], sources[at], index_ref if n == 1 else index_ref.at[c], mats.at[c], w_ref,
            stack_ref, moved_ref, hot_ref, partials[at], fluxes[at], chosen[at],
        )


def step_kernel(n, *refs):
    refs = list(refs)

    def take(count):
        got = refs[:count]
        del refs[:count]
        return got

    ending = [c for c in range(3) if n % 2**c == 0]
    sending = [c for c in range(3) if (n + 1) % 2**c == 0] if n < STEPS else []
    last = n == STEPS
    (dev_ref,) = take(1)
    got = take(3)
    index_ref, orient_ref = take(2)
    (mats,) = take(1)
    w_ref, ow_ref, lw_ref = take(3)
    partials = dict((c, take(1)[0]) for c in ending)
    fluxes = dict((c, take(1)[0]) for c in ending)
    chosen = dict((c, take(1)[0]) for c in ending)
    if last:
        (rank_ref,) = take(1)
        final_ref, energy_ref = take(2)
        news = None
    else:
        kept = dict((c, take(1)[0]) for c in range(3) if c not in ending)
        before = take(3) if n % 2 == 1 else None
        half_sums = take(3) if n == 3 else None
        near_first_ref, place_ref = take(2) if n == 1 else (None, None)
        send_ref = take(1)[0] if n > 1 else None
        news = dict((c, take(1)[0]) for c in ending)
        new_owns = dict((c, take(1)[0]) for c in ending)
        new_traces = dict((c, take(2**c)) for c in ending)
        sums = take(3) if n == 1 else None
        lhs = dict((c, take(1)[0]) for c in sending)
        if n == 1:
            (send_ref,) = take(1)
        out_ref, cross_ref = take(2)
    ghost_ref, stack_ref, moved_ref, hot_ref, gat_ref, cstack_ref, near_ref, flux_ref, fstack_ref = take(9)
    if last:
        (new_scratch,) = take(1)
        news = dict((c, new_scratch.at[c]) for c in range(3))
    else:
        d_ref, msg_ref = take(2)
        if n == 3:
            sums = take(3)
        if n == 1:
            (whole_ref,) = take(1)
    for at, c in enumerate(ending):
        if n == 1:
            unpack_first(
                dev_ref, got, place_ref, send_ref, whole_ref, w_ref, stack_ref, near_ref, ghost_ref
            )
        else:
            unpack(dev_ref, at, got, gat_ref.at[:, 0 : 2 * L], ghost_ref)
        ghost_part(
            partials[c], fluxes[c], chosen[c], ghost_ref, near_first_ref if n == 1 else index_ref.at[c],
            orient_ref.at[c], mats.at[c], ow_ref, lw_ref,
            hot_ref, gat_ref, cstack_ref, near_ref, flux_ref, fstack_ref, news[c],
        )
    if last:
        total = jnp.zeros((8, L), F32)
        for c in range(3):
            for q in range(Q):
                v = news[c][q]
                total = total + jnp.sum((v * v).reshape(B // 8, 8, L), axis=0)
        line = jnp.sum(total, axis=0, keepdims=True)
        energy_ref[...] = jnp.broadcast_to(line[None], energy_ref.shape)
        for b in range(3):
            blk = rows_of(rank_ref[0:1, class_lanes(b)], B)
            index = rows_of(rank_ref[1:2, class_lanes(b)], B)

            def unsort(q, carry):
                final_ref[q, :, class_lanes(b)] = pick([news[c][q] for c in range(3)], blk, index)
                return carry

            lax.fori_loop(0, Q, unsort, 0)
        return
    for c in ending:
        for q in range(Q):
            d_ref[0, q] = news[c][q]
        run_steps(ORDER - 1, mats.at[c], d_ref, w_ref, stack_ref, moved_ref)
        after_steps(c, d_ref, w_ref, stack_ref, new_owns[c], new_traces[c])
    now = [new_traces[c][0] if c in ending else kept[c] for c in range(3)]
    stack_traces(lhs[0], now)
    if sums is not None:
        for b in range(3):
            for q in range(Q):
                sums[b][q] = before[b][q] + now[b][q]
        stack_traces(lhs[1], sums)
    if n == 3:
        for b in range(3):
            for q in range(Q):
                sums[b][q] = sums[b][q] + half_sums[b][q]
        stack_traces(lhs[2], sums)
    pack(dev_ref, [(g, lhs[g]) for g in sending], send_ref, hot_ref, gat_ref, msg_ref, out_ref, cross_ref)


FIELD = (Q, B, L)
TRACE = (Q, 4 * FP, L)


def shards(
    state, class_label, stiffness, star, face_proj, orient_map, flux_local, flux_neigh,
    neighbor, neighbor_face, orientation, send_list,
):
    elements = state.shape[2]
    devices = lax.axis_size("dom")
    aligned = [[GROUP * k + i for i in range(GROUP)] for k in range(devices // GROUP)]
    across = [(d, d + REACH if d % GROUP < REACH else d - REACH) for d in range(devices)]
    onward = [(d, (d + GROUP if d % GROUP < REACH else d - GROUP) % devices) for d in range(devices)]
    axis_index = lax.axis_index("dom").astype(I32)
    exit_first = jnp.where(axis_index % GROUP < REACH, REACH, 0).astype(I32)
    axis_index, exit_first = lax.optimization_barrier((axis_index, exit_first))

    def exchange(out, cross):
        got = lax.all_to_all(out, "dom", 0, 0, axis_index_groups=aligned, tiled=True)
        got, cross = lax.optimization_barrier((got, cross))
        got_cross = lax.ppermute(cross, "dom", across)
        far = lax.dynamic_slice_in_dim(got, exit_first, REACH, 0, allow_negative_indices=False)
        return got, got_cross, lax.ppermute(far, "dom", onward), far

    dev = axis_index.reshape(1)
    smem = pl.BlockSpec(memory_space=pltpu.SMEM)
    whole = pl.BlockSpec(memory_space=pltpu.VMEM)
    stay = pl.BlockSpec(memory_space=pltpu.HBM)

    def run(kernel, args, outs, scratch, name, rest=whole, cost=None):
        return pl.pallas_call(
            kernel,
            in_specs=[smem] + [rest] * (len(args) - 1),
            out_specs=[whole] * len(outs),
            out_shape=outs,
            scratch_shapes=scratch,
            compiler_params=pltpu.CompilerParams(vmem_limit_bytes=VMEM_LIMIT),
            name=name,
            cost_estimate=cost,
        )(*args)

    stack = pltpu.VMEM((192, Q * L), BF16)
    moved = pltpu.VMEM((Q, WROWS, L), F32)
    gat = pltpu.VMEM((TROWS, 4 * L), F32)
    stacked = shape((2 * HALF, SOURCES * L), BF16)

    def hot(blocks):
        return pltpu.VMEM((blocks * L, 4 * L), BF16)

    def msg(count):
        return pltpu.VMEM((PEERS, count, 8, L), F32)

    def messages(rows, count):
        return [shape((GROUP, rows, count, 8, L)), shape((1, rows, count, 8, L))]

    def matrices(array):
        return array.transpose(1, 2, 0, 3)

    inputs = [
        class_label.reshape(3, L), neighbor, neighbor_face, orientation, send_list, stiffness,
        face_proj.transpose(1, 0, 2), orient_map,
        state, matrices(star), matrices(flux_local), matrices(flux_neigh),
    ]
    got = list(
        run(
            first_kernel,
            [dev] + [pltpu.with_memory_space_constraint(x, pltpu.HBM) for x in inputs],
            [shape(FIELD)] * 3 + [shape((3, Q * Q, 16, L))] + [shape(FIELD)] * 3 + [shape(TRACE)] * 7 + [stacked]
            + [shape((3, 8, L), I32), shape((8, L), I32), shape((3, 8, L), I32), shape((8, elements), I32), shape((8, L), I32)]
            + [shape((WROWS, 192), BF16), shape((3 * FP, 96), BF16), shape((288, B), BF16)]
            + messages(1, MSG0),
            [pltpu.VMEM(x.shape, x.dtype) for x in inputs]
            + [
                pltpu.SemaphoreType.DMA((len(inputs),)),
                pltpu.VMEM((8, elements), I32), pltpu.VMEM((8, 2 * L), F32),
                pltpu.VMEM((WROWS, 192), F32), pltpu.VMEM((3 * FP, 96), F32), pltpu.VMEM((288, B), F32),
                pltpu.VMEM((3 * PEERS, L), I32),
                pltpu.VMEM((3, ORDER) + FIELD, F32), stack, moved, pltpu.VMEM((4 * L, 2 * L), BF16),
                pltpu.VMEM((2 * HALF0, 3 * L), BF16), pltpu.VMEM((Q * B, 2 * L), F32), msg(MSG0),
            ],
            "first",
            rest=stay,
        )
    )
    fields = got[0:3]
    mats = got[3]
    owns = got[4:7]
    t00, t10, t11, t20, t21, t22, t23, lhs = got[7:15]
    near, near_first, orient, rank, place, w, ow, lw, out, cross = got[15:]
    later = {1: {0: t10, 1: t11}, 2: {0: t20, 1: t21, 2: t22, 3: t23}}
    now = [t00, t10, t20]
    sources = {0: lhs}
    half_sums = None
    for n in range(1, STEPS + 1):
        ending = [c for c in range(3) if n % 2**c == 0]
        got_out, got_cross, got_far, far = exchange(out, cross)
        count = len(ending)
        parts = list(
            run(
                lambda *refs, n=n: local_kernel(n, *refs),
                [dev, far, near_first if n == 1 else near, mats, w]
                + [fields[c] for c in ending] + [owns[c] for c in ending] + [sources[c] for c in ending],
                [shape(FIELD)] * count + [shape(TRACE)] * count + [shape((TROWS, 4 * L))] * count,
                [stack, moved, pltpu.VMEM((SOURCES * L, 4 * L), BF16)],
                "local%d" % n,
                cost=pl.CostEstimate(flops=count * 3 * 10**9, bytes_accessed=count * 8 * 10**6, transcendentals=0),
            )
        )
        args = [dev, got_out, got_cross, got_far, near, orient, mats, w, ow, lw] + parts
        common = [
            pltpu.VMEM((2 * HALF, (8 if n == 1 else 2) * L), BF16), stack, moved, hot(SOURCES), gat, pltpu.VMEM((96, Q * L), BF16),
            pltpu.VMEM(TRACE, F32), pltpu.VMEM(TRACE, F32), pltpu.VMEM((288, Q * L), BF16),
        ]

        def kernel(*refs, n=n):
            step_kernel(n, *refs)

        if n == STEPS:
            final_state, energy_out = run(
                kernel,
                args + [rank],
                [shape((Q, B, elements)), shape((devices, 1, L))],
                common + [pltpu.VMEM((3,) + FIELD, F32)],
                "last",
            )
            break
        sending = [c for c in range(3) if (n + 1) % 2**c == 0]
        kept = [c for c in range(3) if c not in ending]
        args += [later[c][n % 2**c] for c in kept]
        if n % 2 == 1:
            args += now
        if n == 3:
            args += half_sums
        args += [near_first, place] if n == 1 else [send_index]
        outs = [shape(FIELD)] * (2 * len(ending)) + [shape(TRACE)] * sum(2**c for c in ending)
        outs += [shape(TRACE)] * (3 if n == 1 else 0) + [stacked] * len(sending)
        outs += [shape((8, L), I32)] if n == 1 else []
        outs += messages(len(sending), MSG)
        scratch = common + [pltpu.VMEM((ORDER,) + FIELD, F32), msg(MSG)]
        scratch += [pltpu.VMEM(TRACE, F32)] * (3 if n == 3 else 0)
        scratch += [pltpu.VMEM((2,) + FIELD, F32)] if n == 1 else []
        got = list(run(kernel, args, outs, scratch, "step%d" % n))
        for c in ending:
            fields[c] = got.pop(0)
        for c in ending:
            owns[c] = got.pop(0)
        for c in ending:
            made = [got.pop(0) for _ in range(2**c)]
            later[c] = dict(enumerate(made))
        now = [later[c][n % 2**c] for c in range(3)]
        if n == 1:
            half_sums = [got.pop(0) for _ in range(3)]
        for c in sending:
            sources[c] = got.pop(0)
        if n == 1:
            send_index = got.pop(0)
        out, cross = got
    spread = lax.all_to_all(energy_out, "dom", 0, 0, tiled=True)
    energy = jnp.sum(spread).reshape(1) / (devices * elements * Q * B)
    return final_state, energy


def solution(mesh):
    in_specs = (
        P(None, None, "dom"),
        P("dom"),
        P(),
        P(None, None, None, "dom"),
        P(),
        P(),
        P(None, None, None, "dom"),
        P(None, None, None, "dom"),
        P(None, "dom"),
        P(None, "dom"),
        P(None, "dom"),
        P("dom", None),
    )
    out_specs = (P(None, None, "dom"), P())
    return jax.shard_map(shards, mesh=mesh, in_specs=in_specs, out_specs=out_specs, check_vma=False)
```

```python
import math

import jax
import jax.numpy as jnp
from jax import lax
from jax.experimental import pallas as pl
from jax.experimental.pallas import tpu as pltpu
from jax.sharding import PartitionSpec as P

ORDER = 6
Q = 9
B = 56
FB = 21
FP = 24
L = 128
REACH = 4
PEERS = 8
SLOTS = 32
GROUP = 8
STEPS = 4
OFFSETS = [p - REACH if p < REACH else p - REACH + 1 for p in range(PEERS)]
KROWS = 3 * B
WROWS = KROWS + 4 * FP
MSG = 7
HALF = 224
MSG0 = 16
HALF0 = 512
TILES = 3 * Q
TILES0 = 7 * Q
TROWS = Q * FP
SOURCES = 12
NEIGH = 4
STAR = 8
F32 = jnp.float32
BF16 = jnp.bfloat16
I32 = jnp.int32
VMEM_LIMIT = 40 * 1024 * 1024


def shape(dims, dtype=F32):
    return jax.ShapeDtypeStruct(dims, dtype)


def lane_take(x, index):
    numbers = lax.GatherDimensionNumbers(
        offset_dims=(),
        collapsed_slice_dims=(1,),
        start_index_map=(1,),
        operand_batching_dims=(0,),
        start_indices_batching_dims=(0,),
    )
    return lax.gather(
        x,
        index[..., None],
        numbers,
        slice_sizes=(1, 1),
        mode=lax.GatherScatterMode.PROMISE_IN_BOUNDS,
    )


def pick(blocks, code, lane):
    out = lane_take(blocks[0], lane)
    for k in range(1, len(blocks)):
        out = jnp.where(code == k, lane_take(blocks[k], lane), out)
    return out


def rows_of(vec, rows):
    return jnp.broadcast_to(vec, (rows, L))


def split(values):
    hi = values.astype(BF16)
    lo = (values - hi.astype(F32)).astype(BF16)
    return hi, lo


def put_stack(ref, q, values, rows):
    have = values.shape[0]
    if have < rows:
        values = jnp.concatenate([values, jnp.zeros((rows - have, L), F32)], axis=0)
    hi, lo = split(values)
    cols = slice(q * L, (q + 1) * L)
    ref[0:rows, cols] = hi
    ref[rows : 2 * rows, cols] = lo
    ref[2 * rows : 3 * rows, cols] = hi


def column_tiles():
    return [(t, min(2, Q - t)) for t in range(0, Q, 2)]


def product(weights, stack_ref, store, contract=1):
    for start, count in column_tiles():
        cols = slice(start * L, (start + count) * L)
        out = lax.dot_general(
            weights,
            stack_ref[:, cols],
            (((contract,), (0,)), ((), ())),
            preferred_element_type=F32,
        )
        for j in range(count):
            store(start + j, out[:, j * L : (j + 1) * L])


def mix_groups(total, most):
    groups = []
    at = 0
    while at < total:
        size = min(most, total - at)
        groups.append((at, size))
        at += size
    return groups


def row_bcast(ref, at, row):
    return jnp.broadcast_to(ref[at, pl.ds(row, 1), :], (8, L))[None]


def star_mix(mats_ref, moved_ref, put):
    for r0, rn in mix_groups(B, 32):
        acc = [None] * Q
        for d in range(3):
            for q in range(Q):
                m = moved_ref[q, d * B + r0 : d * B + r0 + rn, :].reshape(rn // 8, 8, L)
                for p in range(Q):
                    term = row_bcast(mats_ref, p * Q + q, STAR + d) * m
                    acc[p] = term if acc[p] is None else acc[p] + term
        for p in range(Q):
            put(p, r0, rn, acc[p].reshape(rn, L))


def class_lanes(c):
    return slice(c * L, (c + 1) * L)


def nt_dot(a, b):
    return lax.dot_general(a, b, (((1,), (1,)), ((), ())), preferred_element_type=F32)


def make_indices(
    label_ref, nbr_ref, face_ref, orient_ref, send_ref, stiff_ref, proj_ref, omap_ref,
    order_ref, rank_ref, near_ref, near_first_ref, sorted_orient_ref, place_ref, want_ref,
    w_ref, ow_ref, lw_ref, wf_ref, owf_ref, lwf_ref, pad_ref,
):
    n_el = nbr_ref.shape[1]
    wf_ref[...] = jnp.zeros_like(wf_ref)
    owf_ref[...] = jnp.zeros_like(owf_ref)
    for d in range(3):
        k = stiff_ref[d]
        hi = k.astype(BF16).astype(F32)
        rows = slice(d * B, (d + 1) * B)
        wf_ref[rows, 0:B] = hi
        wf_ref[rows, 64 : 64 + B] = hi
        wf_ref[rows, 128 : 128 + B] = k - hi
    lwf_ref[...] = jnp.zeros_like(lwf_ref)
    for j in range(4):
        k = proj_ref[:, j, :]
        hi = k.astype(BF16).astype(F32)
        rows = slice(KROWS + j * FP, KROWS + j * FP + FB)
        wf_ref[rows, 0:B] = hi
        wf_ref[rows, 64 : 64 + B] = hi
        wf_ref[rows, 128 : 128 + B] = k - hi
        lwf_ref[j * FP : j * FP + FB, :] = hi
        lwf_ref[96 + j * FP : 96 + j * FP + FB, :] = hi
        lwf_ref[192 + j * FP : 192 + j * FP + FB, :] = k - hi
    for h in range(3):
        k = omap_ref[h]
        hi = k.astype(BF16).astype(F32)
        rows = slice(h * FP, h * FP + FB)
        owf_ref[rows, 0:FB] = hi
        owf_ref[rows, 32 : 32 + FB] = hi
        owf_ref[rows, 64 : 64 + FB] = k - hi
    w_ref[...] = wf_ref[...].astype(BF16)
    ow_ref[...] = owf_ref[...].astype(BF16)
    lw_ref[...] = lwf_ref[...].astype(BF16)
    label = jnp.concatenate([label_ref[c : c + 1, :] for c in range(3)], axis=1)
    classes = lax.broadcasted_iota(I32, (8, n_el), 0)
    hot = (jnp.broadcast_to(label, (8, n_el)) == classes).astype(F32)
    row = lax.broadcasted_iota(I32, (n_el, n_el), 0)
    col = lax.broadcasted_iota(I32, (n_el, n_el), 1)
    before = (row < col).astype(F32).astype(BF16)
    prefix = jnp.dot(hot.astype(BF16), before, preferred_element_type=F32)
    base = classes.astype(F32) * float(L)
    rank = jnp.sum(hot * (prefix + base), axis=0, keepdims=True).astype(I32)
    here = (jnp.broadcast_to(rank, (n_el, n_el)) == row).astype(F32).astype(BF16)
    ids = lax.broadcasted_iota(I32, (8, n_el), 1)
    first = lax.broadcasted_iota(I32, (8, n_el), 0) == 0
    parts = jnp.where(first, ids // L, ids % L).astype(F32).astype(BF16)
    order = nt_dot(parts, here).astype(I32)
    order_ref[...] = order
    rank_ref[...] = jnp.where(first, jnp.broadcast_to(rank >> 7, (8, n_el)), jnp.broadcast_to(rank & 127, (8, n_el)))
    rank_blocks = [rows_of(rank[:, class_lanes(c)], 8) for c in range(3)]
    pad = jnp.zeros((4, n_el), I32)
    tables = [jnp.concatenate([ref[...], pad], axis=0) for ref in (nbr_ref, face_ref, orient_ref)]
    want_ref[...] = jnp.zeros_like(want_ref)
    for c in range(3):
        blk = rows_of(order[0:1, class_lanes(c)], 8)
        lane = rows_of(order[1:2, class_lanes(c)], 8)
        nbr, face, orient = [
            pick([t[:, class_lanes(b)] for b in range(3)], blk, lane) for t in tables
        ]
        ghost = nbr >= n_el
        inside = jnp.where(ghost, 0, nbr)
        place = pick(rank_blocks, inside >> 7, inside & 127)
        slot = jnp.where(ghost, nbr - n_el, 0)
        peer = ((slot >> 5) * 11) >> 5
        slot = peer * SLOTS + (slot & 31)
        near_ref[c] = jnp.where(ghost, SOURCES * L + slot, face * (3 * L) + place)
        sorted_orient_ref[c] = orient
        if c == 0:
            near_first_ref[...] = jnp.where(
                ghost, SOURCES * L + face * (2 * L) + slot, face * (3 * L) + place
            )
        slot = jnp.where(ghost, slot, -1)
        want = jnp.zeros((8, 2 * L), F32)
        target = lax.broadcasted_iota(I32, (2 * L, L), 0)
        for f in range(4):
            match = (jnp.broadcast_to(slot[f : f + 1], (2 * L, L)) == target).astype(F32).astype(BF16)
            value = rows_of(face[f : f + 1], 8).astype(F32).astype(BF16)
            want = want + nt_dot(value, match)
        want_ref[c : c + 1] = want[0:1]
    pad_ref[...] = jnp.zeros_like(pad_ref)
    pad_ref[:, 0:SLOTS] = jnp.maximum(send_ref[...], 0)
    quarter = lax.broadcasted_iota(I32, (1, L), 1) >> 5
    rows = []
    for g in range(3):
        for half in range(2):
            row = jnp.zeros((1, L), I32)
            for k in range(4):
                r = 3 * (4 * half + k) + g
                part = pad_ref[r : r + 1, :]
                part = pltpu.roll(part, SLOTS * k, axis=1) if k else part
                row = jnp.where(quarter == k, part, row)
            rows.append(row)
    send = jnp.concatenate(rows + rows[:2], axis=0)
    place_ref[...] = pick(rank_blocks, send >> 7, send & 127)


def run_steps(count, mats_ref, d_ref, w_ref, stack_ref, moved_ref):
    def body(k, carry):
        for q in range(Q):
            put_stack(stack_ref, q, d_ref[k, q], 64)

        def store(q, out):
            moved_ref[q, 0:KROWS] = out

        product(w_ref[0:KROWS, :], stack_ref, store)

        def put(p, r0, rn, value):
            d_ref[k + 1, p, r0 : r0 + rn, :] = value

        star_mix(mats_ref, moved_ref, put)
        return carry

    lax.fori_loop(0, count, body, 0)


def weights_between(start, end):
    return [(float(end) ** (k + 1) - float(start) ** (k + 1)) / math.factorial(k + 1) for k in range(ORDER)]


def integrate(d_ref, q, start, end):
    total = None
    for k, weight in enumerate(weights_between(start, end)):
        term = d_ref[k, q] * weight
        total = term if total is None else total + term
    return total


def traces(value, w_ref, stack_ref, trace_ref):
    for q in range(Q):
        put_stack(stack_ref, q, value(q), 64)

    def store(q, out):
        trace_ref[q] = out

    product(w_ref[KROWS:WROWS, :], stack_ref, store)


def after_steps(c, d_ref, w_ref, stack_ref, own_ref, trace_refs, later_refs=()):
    for t, trace_ref in enumerate(trace_refs):
        traces(lambda q: integrate(d_ref, q, t, t + 1), w_ref, stack_ref, trace_ref)
    for t, later_ref in enumerate(later_refs, len(trace_refs)):
        for q in range(Q):
            later_ref[q] = integrate(d_ref, q, t, t + 1)
    for q in range(Q):
        own_ref[q] = integrate(d_ref, q, 0, 2**c)


def block_transpose(four, lane):
    a, b, c, d = four
    low = (lane & 64) == 0
    a, c = jnp.where(low, a, pltpu.roll(c, 64, axis=1)), jnp.where(low, pltpu.roll(a, 64, axis=1), c)
    b, d = jnp.where(low, b, pltpu.roll(d, 64, axis=1)), jnp.where(low, pltpu.roll(b, 64, axis=1), d)
    low = (lane & 32) == 0
    a, b = jnp.where(low, a, pltpu.roll(b, 32, axis=1)), jnp.where(low, pltpu.roll(a, 96, axis=1), b)
    c, d = jnp.where(low, c, pltpu.roll(d, 32, axis=1)), jnp.where(low, pltpu.roll(c, 96, axis=1), d)
    return [a, b, c, d]


def one_hot(hot_ref, index_ref, at, count, rows, first=0):
    indices = [jnp.broadcast_to(index_ref[at + f : at + f + 1, :], (2 * L, L)) for f in range(count)]

    def body(i, carry):
        start = pl.multiple_of(i * (2 * L), 2 * L)
        row = lax.broadcasted_iota(I32, (2 * L, L), 0) + (first + start)
        for f in range(count):
            match = indices[f] == row
            hot_ref[pl.ds(start, 2 * L), f * L : (f + 1) * L] = match.astype(F32).astype(BF16)
        return carry

    lax.fori_loop(0, -(-rows // (2 * L)), body, 0)


def stack_rows(ref, at, column, values, apart=HALF):
    hi, lo = split(values)
    rows = values.shape[0]
    cols = pl.ds(pl.multiple_of(column * L, L), L)
    ref[at : at + rows, cols] = hi
    ref[apart + at : apart + at + rows, cols] = lo


def stack_quantities(lhs_ref, trace_ref, j, column):
    rows = pl.ds(pl.multiple_of(j * FP, 8), FP)
    for q in range(0, Q - 1, 2):
        two = jnp.concatenate([trace_ref[q, rows, :], trace_ref[q + 1, rows, :]], axis=0)
        stack_rows(lhs_ref, q * FP, column, two)
    stack_rows(lhs_ref, (Q - 1) * FP, column, trace_ref[Q - 1, rows, :])


def stack_traces(lhs_ref, sources):
    def body(j, carry):
        for b in range(3):
            stack_quantities(lhs_ref, sources[b], j, j * 3 + b)
        return carry

    lax.fori_loop(0, 4, body, 0)


def both(out):
    return out[0:TROWS] + out[HALF : HALF + TROWS]


def send_tiles(dev_ref, at, tile, count, msg_ref, out_ref, cross_ref):
    place_in_group = dev_ref[0] % GROUP
    lane = lax.broadcasted_iota(I32, (8, L), 1)
    for half in range(2):
        for v in range(count):
            four = [tile(count * k + v, half) for k in range(4)]
            for k, value in enumerate(block_transpose(four, lane)):
                msg_ref[4 * half + k, v] = value
    for p in range(PEERS):
        to = place_in_group + OFFSETS[p]
        slot = (to + GROUP) % GROUP
        if abs(OFFSETS[p]) < REACH:
            out_ref[slot, at] = msg_ref[p]
            continue
        within = jnp.logical_and(to >= 0, to < GROUP)

        @pl.when(within)
        def _():
            cross_ref[0, at] = msg_ref[p]

        @pl.when(jnp.logical_not(within))
        def _():
            out_ref[slot, at] = msg_ref[p]


def receive_tiles(dev_ref, at, count, got, put):
    got_ref, cross_ref, far_ref = got
    place_in_group = dev_ref[0] % GROUP
    first = jnp.where(place_in_group < REACH, REACH, 0)
    lane = lax.broadcasted_iota(I32, (8, L), 1)
    for half in range(2):
        found = []
        for k in range(4):
            offset = OFFSETS[4 * half + k]
            source = place_in_group + offset
            within = jnp.logical_and(source >= 0, source < GROUP)
            slot = (source + GROUP) % GROUP
            near = cross_ref[0, at] if abs(offset) == REACH else got_ref[slot, at]
            other = far_ref[jnp.clip(slot - first, 0, REACH - 1), at]
            found.append(jnp.where(within, near, other))
        for v in range(count):
            moved = block_transpose([found[k][v] for k in range(4)], lane)
            for k in range(4):
                put(count * k + v, half, moved[k])


def pack(dev_ref, rows, send_ref, hot_ref, gat_ref, msg_ref, out_ref, cross_ref):
    for at, (g, lhs_ref) in enumerate(rows):
        one_hot(hot_ref, send_ref, 2 * g, 2, SOURCES * L)
        out = jnp.dot(lhs_ref[...], hot_ref[0 : SOURCES * L, 0 : 2 * L], preferred_element_type=F32)
        gat_ref[:, 0 : 2 * L] = both(out)

        def tile(t, half):
            if t < TILES:
                return gat_ref[8 * t : 8 * t + 8, class_lanes(half)]
            return jnp.zeros((8, L), F32)

        send_tiles(dev_ref, at, tile, MSG, msg_ref, out_ref, cross_ref)


def unpack(dev_ref, at, got, gat_ref, ghost_ref):
    def put(t, half, value):
        if t < TILES:
            gat_ref[8 * t : 8 * t + 8, class_lanes(half)] = value

    receive_tiles(dev_ref, at, MSG, got, put)
    for half in range(2):
        stack_rows(ghost_ref, 0, half, gat_ref[:, class_lanes(half)])


def unpack_first(dev_ref, got, place_ref, send_ref, whole_ref, w_ref, stack_ref, trace_ref, ghost_ref):
    def put(t, half, value):
        if t < TILES0:
            whole_ref[half, t // 7, 8 * (t % 7) : 8 * (t % 7) + 8, :] = value
            return
        for g in range(3):
            row = 2 * g + half
            send_ref[row : row + 1] = value[g : g + 1].astype(I32) * (3 * L) + place_ref[row : row + 1]

    receive_tiles(dev_ref, 0, MSG0, got, put)
    send_ref[6:8] = place_ref[6:8]
    for half in range(2):
        traces(lambda q: whole_ref[half, q], w_ref, stack_ref, trace_ref)

        def body(j, carry):
            stack_quantities(ghost_ref, trace_ref, j, 2 * j + half)
            return carry

        lax.fori_loop(0, 4, body, 0)


def flux_mix(mats_ref, row, trace_ref, at, flux_ref, more):
    def body(f, carry):
        r = pl.multiple_of(f * FP, 8)
        acc = [flux_ref[p, pl.ds(r, FP), :].reshape(3, 8, L) if more else None for p in range(Q)]
        for q in range(Q):
            trace = trace_ref[q, pl.ds(at + r, FP), :].reshape(3, 8, L)
            for p in range(Q):
                term = row_bcast(mats_ref, p * Q + q, row + f) * trace
                acc[p] = term if acc[p] is None else acc[p] + term
        for p in range(Q):
            flux_ref[p, pl.ds(r, FP), :] = acc[p].reshape(FP, L)
        return carry

    lax.fori_loop(0, 4, body, 0)


def local_part(
    state_ref, own_ref, lhs_ref, index_ref, mats_ref, w_ref, stack_ref, moved_ref, hot_ref,
    partial_ref, flux_ref, chosen_ref,
):
    for q in range(Q):
        put_stack(stack_ref, q, own_ref[q], 64)

    def store(q, out):
        moved_ref[q] = out

    product(w_ref[...], stack_ref, store)

    def put(p, r0, rn, value):
        partial_ref[p, r0 : r0 + rn, :] = state_ref[p, r0 : r0 + rn, :] + value

    star_mix(mats_ref, moved_ref, put)
    one_hot(hot_ref, index_ref, 0, 4, SOURCES * L)
    chosen_ref[...] = both(jnp.dot(lhs_ref[...], hot_ref[...], preferred_element_type=F32))
    flux_mix(mats_ref, 0, moved_ref, KROWS, flux_ref, False)


def ghost_part(
    partial_ref, flux_ref, chosen_ref, ghost_ref, index_ref, orient_ref, mats_ref, ow_ref, lw_ref,
    hot_ref, gat_ref, cstack_ref, near_ref, sum_ref, fstack_ref, new_ref,
):
    ghosts = ghost_ref.shape[1]
    one_hot(hot_ref, index_ref, 0, 4, ghosts, SOURCES * L)
    out = jnp.dot(ghost_ref[...], hot_ref[0:ghosts, :], preferred_element_type=F32)
    gat_ref[...] = chosen_ref[...] + both(out)
    for f in range(4):
        for q in range(Q):
            put_stack(cstack_ref, q, gat_ref[q * FP : (q + 1) * FP, f * L : (f + 1) * L], 32)
        turn = rows_of(orient_ref[f : f + 1, :], FP)

        def store_near(q, out):
            value = jnp.where(turn == 1, out[FP : 2 * FP], out[0:FP])
            near_ref[q, f * FP : (f + 1) * FP] = jnp.where(turn == 2, out[2 * FP :], value)

        product(ow_ref[...], cstack_ref, store_near)
    sum_ref[...] = flux_ref[...]
    flux_mix(mats_ref, NEIGH, near_ref, 0, sum_ref, True)
    for p in range(Q):
        put_stack(fstack_ref, p, sum_ref[p], 96)

    def subtract(p, out):
        new_ref[p] = partial_ref[p] - out

    product(lw_ref[...], fstack_ref, subtract, contract=0)


def first_kernel(*refs):
    dev_ref = refs[0]
    hbm = refs[1:13]
    (
        s0, s1, s2, mats, own0, own1, own2, t00, t10, t20, j11, j21, j22, j23,
        near_ref, near_first_ref, sorted_orient_ref, rank_ref, place_ref, w_ref, ow_ref, lw_ref,
        out_ref, cross_ref,
    ) = refs[13:37]
    local = refs[37:49]
    (
        sems, order_ref, want_ref, wf_ref, owf_ref, lwf_ref, pad_ref,
        d_ref, stack_ref, moved_ref, hot_ref, jl_ref, gat_ref, msg_ref,
    ) = refs[49:]
    copies = [pltpu.make_async_copy(a, b, sems.at[i]) for i, (a, b) in enumerate(zip(hbm, local))]
    for copy in copies:
        copy.start()
    for copy in copies[:8]:
        copy.wait()
    make_indices(
        *local[:8], order_ref, rank_ref, near_ref, near_first_ref, sorted_orient_ref, place_ref, want_ref,
        w_ref, ow_ref, lw_ref, wf_ref, owf_ref, lwf_ref, pad_ref,
    )
    for copy in copies[8:]:
        copy.wait()
    state_ref, star_ref, fl_ref, fn_ref = local[8:]
    picks = []
    for c in range(3):
        picks.append((order_ref[0:1, class_lanes(c)], order_ref[1:2, class_lanes(c)]))
    states = [s0, s1, s2]

    def sort_rows(blocks, put):
        rows = blocks[0].shape[0]
        for c in range(3):
            put(c, pick(blocks, rows_of(picks[c][0], rows), rows_of(picks[c][1], rows)))

    def sort_state(q, carry):
        def put(c, value):
            states[c][q] = value
            d_ref[c, 0, q] = value

        sort_rows([state_ref[q, :, class_lanes(b)] for b in range(3)], put)
        return carry

    lax.fori_loop(0, Q, sort_state, 0)

    def sort_matrices(p, carry):
        for q in range(Q):
            at = p * Q + q

            def put_flux(c, value):
                mats[c, at, 0:8, :] = value

            def put_star(c, value):
                mats[c, at, STAR : STAR + 3, :] = value

            sort_rows(
                [
                    jnp.concatenate([fl_ref[p, q, :, class_lanes(b)], fn_ref[p, q, :, class_lanes(b)]], axis=0)
                    for b in range(3)
                ],
                put_flux,
            )
            sort_rows([star_ref[p, q, :, class_lanes(b)] for b in range(3)], put_star)
        return carry

    lax.fori_loop(0, Q, sort_matrices, 0)

    def each(c, carry):
        run_steps(ORDER - 1, mats.at[c], d_ref.at[c], w_ref, stack_ref, moved_ref)
        return carry

    lax.fori_loop(0, 3, each, 0)
    after_steps(0, d_ref.at[0], w_ref, stack_ref, own0, [t00])
    after_steps(1, d_ref.at[1], w_ref, stack_ref, own1, [t10], [j11])
    after_steps(2, d_ref.at[2], w_ref, stack_ref, own2, [t20], [j21, j22, j23])
    for c in range(3):
        for q in range(0, Q, 2):
            parts = [integrate(d_ref.at[c], r, 0, 1) for r in range(q, min(q + 2, Q))]
            stack_rows(jl_ref, q * B, c, jnp.concatenate(parts, axis=0), HALF0)
    one_hot(hot_ref, place_ref, 0, 2, 3 * L)
    out = jnp.dot(jl_ref[...], hot_ref[0 : 3 * L, 0 : 2 * L], preferred_element_type=F32)
    gat_ref[...] = out[0 : Q * B] + out[HALF0 : HALF0 + Q * B]

    def tile(t, half):
        if t < TILES0:
            return gat_ref[8 * t : 8 * t + 8, class_lanes(half)]
        return want_ref[:, class_lanes(half)]

    send_tiles(dev_ref, 0, tile, MSG0, msg_ref, out_ref, cross_ref)


def local_kernel(n, *refs):
    refs = list(refs)

    def take(count):
        got = refs[:count]
        del refs[:count]
        return got

    ending = [c for c in range(3) if n % 2**c == 0]
    take(2)
    index_ref, mats, w_ref = take(3)
    states, owns, sources = take(len(ending)), take(len(ending)), take(3 if n == 1 else len(ending))
    later = take(4) if n == 1 else []
    partials, fluxes, chosen = take(len(ending)), take(len(ending)), take(len(ending))
    later_traces = take(4) if n == 1 else []
    made_lhs = take(1) if n == 1 else None
    stack_ref, moved_ref, hot_ref = take(3)
    for value_ref, trace_ref in zip(later, later_traces):
        traces(lambda q: value_ref[q], w_ref, stack_ref, trace_ref)
    if n == 1:
        stack_traces(made_lhs[0], sources)
        sources = made_lhs
    for at, c in enumerate(ending):
        local_part(
            states[at], owns[at], sources[at], index_ref if n == 1 else index_ref.at[c], mats.at[c], w_ref,
            stack_ref, moved_ref, hot_ref, partials[at], fluxes[at], chosen[at],
        )


def step_kernel(n, *refs):
    refs = list(refs)

    def take(count):
        got = refs[:count]
        del refs[:count]
        return got

    ending = [c for c in range(3) if n % 2**c == 0]
    sending = [c for c in range(3) if (n + 1) % 2**c == 0] if n < STEPS else []
    last = n == STEPS
    (dev_ref,) = take(1)
    got = take(3)
    index_ref, orient_ref = take(2)
    (mats,) = take(1)
    w_ref, ow_ref, lw_ref = take(3)
    partials = dict((c, take(1)[0]) for c in ending)
    fluxes = dict((c, take(1)[0]) for c in ending)
    chosen = dict((c, take(1)[0]) for c in ending)
    if last:
        (rank_ref,) = take(1)
        final_ref, energy_ref = take(2)
        news = None
    else:
        kept = dict((c, take(1)[0]) for c in range(3) if c not in ending)
        before = take(3) if n % 2 == 1 else None
        half_sums = take(3) if n == 3 else None
        near_first_ref, place_ref = take(2) if n == 1 else (None, None)
        send_ref = take(1)[0] if n > 1 else None
        news = dict((c, take(1)[0]) for c in ending)
        new_owns = dict((c, take(1)[0]) for c in ending)
        new_traces = dict((c, take(2**c)) for c in ending)
        sums = take(3) if n == 1 else None
        lhs = dict((c, take(1)[0]) for c in sending)
        if n == 1:
            (send_ref,) = take(1)
        out_ref, cross_ref = take(2)
    ghost_ref, stack_ref, moved_ref, hot_ref, gat_ref, cstack_ref, near_ref, flux_ref, fstack_ref = take(9)
    if last:
        (new_scratch,) = take(1)
        news = dict((c, new_scratch.at[c]) for c in range(3))
    else:
        d_ref, msg_ref = take(2)
        if n == 3:
            sums = take(3)
        if n == 1:
            (whole_ref,) = take(1)
    for at, c in enumerate(ending):
        if n == 1:
            unpack_first(
                dev_ref, got, place_ref, send_ref, whole_ref, w_ref, stack_ref, near_ref, ghost_ref
            )
        else:
            unpack(dev_ref, at, got, gat_ref.at[:, 0 : 2 * L], ghost_ref)
        ghost_part(
            partials[c], fluxes[c], chosen[c], ghost_ref, near_first_ref if n == 1 else index_ref.at[c],
            orient_ref.at[c], mats.at[c], ow_ref, lw_ref,
            hot_ref, gat_ref, cstack_ref, near_ref, flux_ref, fstack_ref, news[c],
        )
    if last:
        total = jnp.zeros((8, L), F32)
        for c in range(3):
            for q in range(Q):
                v = news[c][q]
                total = total + jnp.sum((v * v).reshape(B // 8, 8, L), axis=0)
        line = jnp.sum(total, axis=0, keepdims=True)
        energy_ref[...] = jnp.broadcast_to(line[None], energy_ref.shape)
        for b in range(3):
            blk = rows_of(rank_ref[0:1, class_lanes(b)], B)
            index = rows_of(rank_ref[1:2, class_lanes(b)], B)

            def unsort(q, carry):
                final_ref[q, :, class_lanes(b)] = pick([news[c][q] for c in range(3)], blk, index)
                return carry

            lax.fori_loop(0, Q, unsort, 0)
        return
    for c in ending:
        for q in range(Q):
            d_ref[0, q] = news[c][q]
        run_steps(ORDER - 1, mats.at[c], d_ref, w_ref, stack_ref, moved_ref)
        after_steps(c, d_ref, w_ref, stack_ref, new_owns[c], new_traces[c])
    now = [new_traces[c][0] if c in ending else kept[c] for c in range(3)]
    stack_traces(lhs[0], now)
    if sums is not None:
        for b in range(3):
            for q in range(Q):
                sums[b][q] = before[b][q] + now[b][q]
        stack_traces(lhs[1], sums)
    if n == 3:
        for b in range(3):
            for q in range(Q):
                sums[b][q] = sums[b][q] + half_sums[b][q]
        stack_traces(lhs[2], sums)
    pack(dev_ref, [(g, lhs[g]) for g in sending], send_ref, hot_ref, gat_ref, msg_ref, out_ref, cross_ref)


FIELD = (Q, B, L)
TRACE = (Q, 4 * FP, L)


def shards(
    state, class_label, stiffness, star, face_proj, orient_map, flux_local, flux_neigh,
    neighbor, neighbor_face, orientation, send_list,
):
    elements = state.shape[2]
    devices = lax.axis_size("dom")
    aligned = [[GROUP * k + i for i in range(GROUP)] for k in range(devices // GROUP)]
    across = [(d, d + REACH if d % GROUP < REACH else d - REACH) for d in range(devices)]
    onward = [(d, (d + GROUP if d % GROUP < REACH else d - GROUP) % devices) for d in range(devices)]
    axis_index = lax.axis_index("dom").astype(I32)
    exit_first = jnp.where(axis_index % GROUP < REACH, REACH, 0).astype(I32)
    axis_index, exit_first = lax.optimization_barrier((axis_index, exit_first))

    def exchange(out, cross):
        got = lax.all_to_all(out, "dom", 0, 0, axis_index_groups=aligned, tiled=True)
        far = lax.dynamic_slice_in_dim(got, exit_first, REACH, 0, allow_negative_indices=False)
        far, cross = lax.optimization_barrier((far, cross))
        got_far = lax.ppermute(far, "dom", onward)
        got_cross = lax.ppermute(cross, "dom", across)
        return got, got_cross, got_far, far

    dev = axis_index.reshape(1)
    smem = pl.BlockSpec(memory_space=pltpu.SMEM)
    whole = pl.BlockSpec(memory_space=pltpu.VMEM)
    stay = pl.BlockSpec(memory_space=pltpu.HBM)

    def run(kernel, args, outs, scratch, name, rest=whole, cost=None):
        return pl.pallas_call(
            kernel,
            in_specs=[smem] + [rest] * (len(args) - 1),
            out_specs=[whole] * len(outs),
            out_shape=outs,
            scratch_shapes=scratch,
            compiler_params=pltpu.CompilerParams(vmem_limit_bytes=VMEM_LIMIT),
            name=name,
            cost_estimate=cost,
        )(*args)

    stack = pltpu.VMEM((192, Q * L), BF16)
    moved = pltpu.VMEM((Q, WROWS, L), F32)
    gat = pltpu.VMEM((TROWS, 4 * L), F32)
    stacked = shape((2 * HALF, SOURCES * L), BF16)

    def hot(blocks):
        return pltpu.VMEM((blocks * L, 4 * L), BF16)

    def msg(count):
        return pltpu.VMEM((PEERS, count, 8, L), F32)

    def messages(rows, count):
        return [shape((GROUP, rows, count, 8, L)), shape((1, rows, count, 8, L))]

    def matrices(array):
        return array.transpose(1, 2, 0, 3)

    inputs = [
        class_label.reshape(3, L), neighbor, neighbor_face, orientation, send_list, stiffness,
        face_proj.transpose(1, 0, 2), orient_map,
        state, matrices(star), matrices(flux_local), matrices(flux_neigh),
    ]
    got = list(
        run(
            first_kernel,
            [dev] + [pltpu.with_memory_space_constraint(x, pltpu.HBM) for x in inputs],
            [shape(FIELD)] * 3 + [shape((3, Q * Q, 16, L))] + [shape(FIELD)] * 3 + [shape(TRACE)] * 3 + [shape(FIELD)] * 4
            + [shape((3, 8, L), I32), shape((8, L), I32), shape((3, 8, L), I32), shape((8, elements), I32), shape((8, L), I32)]
            + [shape((WROWS, 192), BF16), shape((3 * FP, 96), BF16), shape((288, B), BF16)]
            + messages(1, MSG0),
            [pltpu.VMEM(x.shape, x.dtype) for x in inputs]
            + [
                pltpu.SemaphoreType.DMA((len(inputs),)),
                pltpu.VMEM((8, elements), I32), pltpu.VMEM((8, 2 * L), F32),
                pltpu.VMEM((WROWS, 192), F32), pltpu.VMEM((3 * FP, 96), F32), pltpu.VMEM((288, B), F32),
                pltpu.VMEM((3 * PEERS, L), I32),
                pltpu.VMEM((3, ORDER) + FIELD, F32), stack, moved, pltpu.VMEM((4 * L, 2 * L), BF16),
                pltpu.VMEM((2 * HALF0, 3 * L), BF16), pltpu.VMEM((Q * B, 2 * L), F32), msg(MSG0),
            ],
            "first",
            rest=stay,
        )
    )
    fields = got[0:3]
    mats = got[3]
    owns = got[4:7]
    now = got[7:10]
    integrals = got[10:14]
    near, near_first, orient, rank, place, w, ow, lw, out, cross = got[14:]
    later = None
    sources = {}
    half_sums = None
    for n in range(1, STEPS + 1):
        ending = [c for c in range(3) if n % 2**c == 0]
        got_out, got_cross, got_far, far = exchange(out, cross)
        count = len(ending)
        parts = list(
            run(
                lambda *refs, n=n: local_kernel(n, *refs),
                [dev, far, near_first if n == 1 else near, mats, w]
                + [fields[c] for c in ending] + [owns[c] for c in ending]
                + (now + integrals if n == 1 else [sources[c] for c in ending]),
                [shape(FIELD)] * count + [shape(TRACE)] * count + [shape((TROWS, 4 * L))] * count
                + ([shape(TRACE)] * 4 + [stacked] if n == 1 else []),
                [stack, moved, pltpu.VMEM((SOURCES * L, 4 * L), BF16)],
                "local%d" % n,
                cost=pl.CostEstimate(flops=count * 3 * 10**9, bytes_accessed=count * 8 * 10**6, transcendentals=0),
            )
        )
        if n == 1:
            t11, t21, t22, t23 = parts[3:7]
            later = {1: {0: now[1], 1: t11}, 2: {0: now[2], 1: t21, 2: t22, 3: t23}}
            parts = parts[:3]
        args = [dev, got_out, got_cross, got_far, near, orient, mats, w, ow, lw] + parts
        common = [
            pltpu.VMEM((2 * HALF, (8 if n == 1 else 2) * L), BF16), stack, moved, hot(SOURCES), gat, pltpu.VMEM((96, Q * L), BF16),
            pltpu.VMEM(TRACE, F32), pltpu.VMEM(TRACE, F32), pltpu.VMEM((288, Q * L), BF16),
        ]

        def kernel(*refs, n=n):
            step_kernel(n, *refs)

        if n == STEPS:
            final_state, energy_out = run(
                kernel,
                args + [rank],
                [shape((Q, B, elements)), shape((devices, 1, L))],
                common + [pltpu.VMEM((3,) + FIELD, F32)],
                "last",
            )
            break
        sending = [c for c in range(3) if (n + 1) % 2**c == 0]
        kept = [c for c in range(3) if c not in ending]
        args += [later[c][n % 2**c] for c in kept]
        if n % 2 == 1:
            args += now
        if n == 3:
            args += half_sums
        args += [near_first, place] if n == 1 else [send_index]
        outs = [shape(FIELD)] * (2 * len(ending)) + [shape(TRACE)] * sum(2**c for c in ending)
        outs += [shape(TRACE)] * (3 if n == 1 else 0) + [stacked] * len(sending)
        outs += [shape((8, L), I32)] if n == 1 else []
        outs += messages(len(sending), MSG)
        scratch = common + [pltpu.VMEM((ORDER,) + FIELD, F32), msg(MSG)]
        scratch += [pltpu.VMEM(TRACE, F32)] * (3 if n == 3 else 0)
        scratch += [pltpu.VMEM((2,) + FIELD, F32)] if n == 1 else []
        got = list(run(kernel, args, outs, scratch, "step%d" % n))
        for c in ending:
            fields[c] = got.pop(0)
        for c in ending:
            owns[c] = got.pop(0)
        for c in ending:
            made = [got.pop(0) for _ in range(2**c)]
            later[c] = dict(enumerate(made))
        now = [later[c][n % 2**c] for c in range(3)]
        if n == 1:
            half_sums = [got.pop(0) for _ in range(3)]
        for c in sending:
            sources[c] = got.pop(0)
        if n == 1:
            send_index = got.pop(0)
        out, cross = got
    spread = lax.all_to_all(energy_out, "dom", 0, 0, tiled=True)
    energy = jnp.sum(spread).reshape(1) / (devices * elements * Q * B)
    return final_state, energy


def solution(mesh):
    in_specs = (
        P(None, None, "dom"),
        P("dom"),
        P(),
        P(None, None, None, "dom"),
        P(),
        P(),
        P(None, None, None, "dom"),
        P(None, None, None, "dom"),
        P(None, "dom"),
        P(None, "dom"),
        P(None, "dom"),
        P("dom", None),
    )
    out_specs = (P(None, None, "dom"), P())
    return jax.shard_map(shards, mesh=mesh, in_specs=in_specs, out_specs=out_specs, check_vma=False)
```
